1024 devices in a mesh: dp: 16 (over z), expert: 16 (over y, core), tensor: 4 (over x).
Axes of the slice: x: 4, y: 8, z: 16, core: 2. Of those that a mesh axis runs over, the one named last changes fastest.
Arguments:
- tokens: bfloat16 [4096, 2048], P(('dp', 'expert', 'tensor')), may hold values from -6 to 6
- routes: int32 [4096, 6], P(('dp', 'expert')), may hold values from 0 to 15, as said below
- positions: int32 [4096, 6], P(('dp', 'expert')), may hold values from 0 to 7, as said below
- combine_weights: float32 [4096, 6], P(('dp', 'expert')), may hold values from 0.1 to 1
- cotangent: bfloat16 [4096, 2048], P(('dp', 'expert', 'tensor')), may hold values from -6 to 6
- gate_weight: bfloat16 [16, 2048, 1408], P('expert', None, 'tensor'), may hold values from -0.125 to 0.125
- up_weight: bfloat16 [16, 2048, 1408], P('expert', None, 'tensor'), may hold values from -0.125 to 0.125
- down_weight: bfloat16 [16, 2048, 1408], P('expert', None, 'tensor'), may hold values from -0.15625 to 0.15625
Outputs:
- layer_out: bfloat16 [4096, 2048], P(('dp', 'expert', 'tensor'))
- grad_tokens: bfloat16 [4096, 2048], P(('dp', 'expert', 'tensor'))
- grad_down: bfloat16 [16, 2048, 1408], P('expert', 'dp', 'tensor')
The draws below stay inside these ranges and needn't reach their ends.
Inputs may be any that keep to these rules, and one draw needn't show every extreme that they name: `routes`: each row names 6 different experts. Within each aligned block of 16 rows, no expert is named by more than 8 rows, and one expert, the same in every block, is named by exactly 8 rows. `positions`: within each aligned block of 16 rows, no two choices share both expert and position.
All inputs are finite; a program needn't handle non-finite values.
Results may differ from the reference program's by a relative error of at most 0.017.
Values may be sent and summed in bfloat16 or wider, within the bound.
A program may use at most 32 MiB of HBM per device.

```python
import math
import jax
import jax.numpy as jnp
from jax import lax

D = 2048
FF = 1408
TOP = 6
EXPERTS = 16
GROUP = 16
CAP = 8
TOKENS = 4096
N_DP = 16
N_EXPERT = 16
N_TENSOR = 4


def route_plan(key):
    blocks = TOKENS // GROUP
    slot_count = EXPERTS * CAP
    extra = TOP * GROUP - CAP
    base_key = jax.random.fold_in(key, 7)
    full_expert = jax.random.randint(jax.random.fold_in(base_key, 1), (), 0, EXPERTS)

    def one_block(block_key):
        order_key, slot_key = jax.random.split(block_key)
        ranks = jax.random.permutation(order_key, EXPERTS).astype(jnp.int32)
        ranks = jnp.where(jnp.arange(EXPERTS, dtype=jnp.int32) == full_expert, -1, ranks)
        ordering = jnp.argsort(ranks).astype(jnp.int32)
        chosen_rest = jax.random.permutation(slot_key, slot_count - CAP)[:extra].astype(jnp.int32) + CAP
        chosen = jnp.sort(jnp.concatenate([jnp.arange(CAP, dtype=jnp.int32), chosen_rest]))
        layout = chosen.reshape(TOP, GROUP).T
        return (ordering[layout // CAP], layout % CAP)
    block_keys = jax.random.split(jax.random.fold_in(base_key, 2), blocks)
    experts_drawn, places_drawn = jax.vmap(one_block)(block_keys)
    return (experts_drawn.reshape(TOKENS, TOP).astype(jnp.int32), places_drawn.reshape(TOKENS, TOP).astype(jnp.int32))


def draw_routes(key, part):
    return route_plan(key)[0]


def draw_positions(key, part):
    return route_plan(key)[1]


def block_scale(key, shape, shards, low, high):
    loudness = 1.0
    for axis_at, blocks in shards:
        steps = jax.random.uniform(jax.random.fold_in(jax.random.fold_in(key, 6), axis_at), (blocks,), jnp.float32, low / len(shards), high / len(shards))
        loudness = loudness * jnp.repeat(jnp.exp(steps), shape[axis_at] // blocks).reshape((-1,) + (1,) * (len(shape) - 1 - axis_at))
    return loudness


def normal_values(own_key, shape, scale, bound, shards=(), kind=jnp.bfloat16):
    drawn = jax.random.normal(own_key, shape, jnp.float32) * scale
    if len(shards) > 0:
        drawn = block_scale(own_key, shape, shards, -0.22, 0.18) * drawn
    return jnp.clip(drawn, min=-bound, max=bound).astype(kind)


def setup_inputs(seed: int = 0) -> dict:
    keys = jax.random.split(jax.random.key(seed), 9)
    return {
        "tokens": normal_values(keys[0], (TOKENS, D), 1.0, 6.0, ((0, 1024),)),
        "routes": draw_routes(jax.random.fold_in(keys[8], 71), 0),
        "positions": draw_positions(jax.random.fold_in(keys[8], 71), 0),
        "combine_weights": jnp.clip(jnp.exp(math.log(1.0) - 2.3025851 * jax.random.uniform(keys[3], (TOKENS, TOP), jnp.float32) ** block_scale(keys[3], (TOKENS, TOP), ((0, 256),), -0.2, 0.2)), 0.1, 1.0),
        "cotangent": normal_values(keys[4], (TOKENS, D), 1.0, 6.0, ((0, 1024),)),
        "gate_weight": normal_values(keys[5], (EXPERTS, D, FF), D ** -0.5, 0.125, ((0, 16), (2, 4))),
        "up_weight": normal_values(keys[6], (EXPERTS, D, FF), D ** -0.5, 0.125, ((0, 16), (2, 4))),
        "down_weight": normal_values(keys[7], (EXPERTS, D, FF), FF ** -0.5, 0.15625, ((0, 16), (2, 4))),
    }


def expert_terms(carry, items):
    slot_back, activation = items
    term = jnp.einsum("erd,erf->edf", slot_back.astype(jnp.float32), activation.astype(jnp.float32), precision=lax.Precision.HIGHEST)
    return carry + lax.optimization_barrier(term.astype(jnp.bfloat16)).astype(jnp.float32), None


def reference(tokens, routes, positions, combine_weights, cotangent, gate_weight, up_weight, down_weight):
    groups = tokens.shape[0] // GROUP
    width = tokens.shape[1]
    slot_count = EXPERTS * CAP
    quarter = FF // N_TENSOR
    highest = lax.Precision.HIGHEST
    slot_index = (routes * CAP + positions).reshape(groups, GROUP, TOP)
    probs = combine_weights.reshape(groups, GROUP, TOP)
    matches = (slot_index[:, :, :, None] == jnp.arange(slot_count, dtype=jnp.int32)).astype(jnp.float32)
    placed = jnp.sum(matches, axis=2)
    weighted = jnp.sum(matches * probs[:, :, :, None], axis=2)
    slot_gain = jnp.sum(weighted, axis=1)

    def to_slots(rows):
        grouped = rows.astype(jnp.float32).reshape(groups, GROUP, width)
        return jnp.einsum("gts,gtd->gsd", placed, grouped, precision=highest)

    def by_expert(slots):
        return slots.reshape(groups, EXPERTS, CAP, -1).transpose(1, 0, 2, 3).reshape(EXPERTS, groups * CAP, -1)

    def by_group(slots):
        return slots.reshape(EXPERTS, groups, CAP, -1).transpose(1, 0, 2, 3).reshape(groups, slot_count, -1)

    def project(left, right):
        return jnp.einsum("erd,edf->erf", left.astype(jnp.float32), right.astype(jnp.float32), precision=highest)

    def by_quarter(left, right):
        left_blocks = left.astype(jnp.float32).reshape(EXPERTS, -1, N_TENSOR, quarter)
        right_blocks = right.astype(jnp.float32).reshape(EXPERTS, width, N_TENSOR, quarter)
        return jnp.einsum("erqf,edqf->qerd", left_blocks, right_blocks, precision=highest)

    def block_sum(parts):
        return jnp.sum(lax.optimization_barrier(parts.astype(jnp.bfloat16)).astype(jnp.float32), axis=0)

    dispatched = by_expert(to_slots(tokens)).astype(jnp.bfloat16)
    gate_pre = project(dispatched, gate_weight)
    up_pre = project(dispatched, up_weight)
    activation = (jax.nn.silu(gate_pre) * up_pre).astype(jnp.bfloat16)
    expert_out = by_group(block_sum(by_quarter(activation, down_weight)))
    layer_out = jnp.einsum("gts,gsd->gtd", weighted, expert_out, precision=highest)
    layer_out = layer_out.reshape(tokens.shape[0], width).astype(jnp.bfloat16)

    slot_cotangent = by_expert(to_slots(cotangent) * slot_gain[:, :, None]).astype(jnp.bfloat16)
    act_grad = jnp.einsum("erd,edf->erf", slot_cotangent.astype(jnp.float32), down_weight.astype(jnp.float32), precision=highest)
    squash = jax.nn.sigmoid(gate_pre)
    gate_back = (act_grad * up_pre * squash * (1.0 + gate_pre * (1.0 - squash))).astype(jnp.bfloat16)
    up_back = (act_grad * jax.nn.silu(gate_pre)).astype(jnp.bfloat16)
    input_part = by_quarter(gate_back, gate_weight) + by_quarter(up_back, up_weight)
    input_slots = by_group(block_sum(input_part))
    grad_tokens = jnp.einsum("gts,gsd->gtd", placed, input_slots, precision=highest)
    grad_tokens = grad_tokens.reshape(tokens.shape[0], width).astype(jnp.bfloat16)

    def split(values):
        return values.reshape(EXPERTS, N_DP, N_EXPERT * CAP, -1).transpose(1, 0, 2, 3)

    zeros = jnp.zeros((EXPERTS, width, FF), jnp.float32)
    total, unused = lax.scan(expert_terms, zeros, (split(slot_cotangent), split(activation)))
    grad_down = (total * (1.0 / N_DP)).astype(jnp.bfloat16)
    return (layer_out, grad_tokens, grad_down)
```

```python
import functools

import jax
import jax.numpy as jnp
from jax import lax
from jax.experimental import pallas as pl
from jax.experimental.pallas import tpu as pltpu
from jax.sharding import PartitionSpec as P

MESH = pl.DeviceIdType.MESH
F32 = jnp.float32
BF16 = jnp.bfloat16
SUB = 4


def dot(left, right):
    return lax.dot_general(left, right, (((1,), (0,)), ((), ())), preferred_element_type=F32)


def dot_t(left, right):
    return lax.dot_general(left, right, (((1,), (1,)), ((), ())), preferred_element_type=F32)


def kernel(
    n_z,
    n_e,
    tok_ref,
    cot_ref,
    routes_ref,
    pos_ref,
    cw_ref,
    gw_hbm,
    uw_hbm,
    dw_hbm,
    lo_ref,
    gt_ref,
    gd_ref,
    gw,
    uw,
    dw,
    xin,
    group,
    dsend,
    rows,
    gate_s,
    up_s,
    part,
    rs_far,
    rs_sum,
    rs_near,
    ysend,
    yret,
    csend,
    fin,
    term,
    zin,
    zout,
    w_sem,
    sx_sem,
    rx_sem,
    sd_sem,
    rd_sem,
    sg_sem,
    rg_sem,
    sr_sem,
    rr_sem,
    sy_sem,
    ry_sem,
    sc_sem,
    rc_sem,
    sz_sem,
    rz_sem,
):
    n_x, _, _, cap, q_cols = rows.shape[1:]
    tokens_here = tok_ref.shape[0]
    group_size = routes_ref.shape[0]
    n_slots = n_e * cap
    half_e = n_e // 2
    half_z = n_z // 2
    hidden = gate_s.shape[1]
    x = lax.axis_index("tensor")
    e = lax.axis_index("expert")
    z = lax.axis_index("dp")

    def x_at(d):
        return lax.rem(x + d + n_x, n_x)

    def e_at(d):
        return lax.rem(e + d + n_e, n_e)

    def z_at(d):
        return lax.rem(z + d + 2 * n_z, n_z)

    started = []

    def send(src, dst, send_sem, recv_sem, device):
        copy = pltpu.make_async_remote_copy(
            src_ref=src,
            dst_ref=dst,
            send_sem=send_sem,
            recv_sem=recv_sem,
            device_id=device,
            device_id_type=MESH,
        )
        copy.start()
        started.append(copy)

    def arrive(dst, send_sem, recv_sem, device):
        pltpu.make_async_remote_copy(
            src_ref=dst,
            dst_ref=dst,
            send_sem=send_sem,
            recv_sem=recv_sem,
            device_id=device,
            device_id_type=MESH,
        ).wait_recv()

    loads = []
    for i, (src, dst) in enumerate(((gw_hbm, gw), (uw_hbm, uw), (dw_hbm, dw))):
        load = pltpu.make_async_copy(src, dst, w_sem.at[i])
        load.start()
        loads.append(load)

    barrier = pltpu.get_barrier_semaphore()
    for d in range(1, n_x):
        pl.semaphore_signal(barrier, inc=1, device_id={"tensor": x_at(d)}, device_id_type=MESH)
    for d in range(1, n_e):
        pl.semaphore_signal(barrier, inc=1, device_id={"expert": e_at(d)}, device_id_type=MESH)
    for d in (1, -1):
        pl.semaphore_signal(barrier, inc=1, device_id={"dp": z_at(d)}, device_id_type=MESH)
    pl.semaphore_wait(barrier, n_x - 1 + n_e - 1 + 2)

    sources = (tok_ref, cot_ref)

    def quarter_of(a, q):
        return sources[a].at[:, pl.ds(pl.multiple_of(q * q_cols, q_cols), q_cols)]

    for a in range(2):
        for d in range(1, n_x):
            q = x_at(d)
            send(
                quarter_of(a, q),
                xin.at[a, x],
                sx_sem.at[a, d],
                rx_sem.at[a, d],
                {"tensor": q},
            )
    for a in range(2):
        xin[a, x] = quarter_of(a, x)[...]

    slot_ids = routes_ref[...] * cap + pos_ref[...]
    gains = cw_ref[...]
    lanes = lax.broadcasted_iota(jnp.int32, (group_size, n_slots), 1)
    placed = jnp.zeros((group_size, n_slots), F32)
    weighted = jnp.zeros((group_size, n_slots), F32)
    for k in range(slot_ids.shape[1]):
        match = lanes == slot_ids[:, k : k + 1]
        placed = placed + jnp.where(match, 1.0, 0.0)
        weighted = weighted + jnp.where(match, gains[:, k : k + 1], 0.0)

    def pieces(table):
        high = table.astype(BF16)
        return high, (table - high.astype(F32)).astype(BF16)

    placed_in = placed.T.astype(BF16)
    weighted_in = pieces(weighted.T)
    placed_back = placed.astype(BF16)
    weighted_back = pieces(weighted)

    def dispatch(a):
        for d in range(1, n_x):
            src = x_at(-d)
            arrive(xin.at[a, src], sx_sem.at[a, d], rx_sem.at[a, d], {"tensor": src})
        for j in range(n_x):
            group[pl.ds(j * tokens_here, tokens_here), :] = xin[a, j].astype(F32)
        here = group[...].astype(BF16)
        if a == 0:
            slots = dot(placed_in, here)
        else:
            slots = dot(weighted_in[0], here) + dot(weighted_in[1], here)
        dsend[a] = slots.reshape(n_e, cap, q_cols).astype(BF16).reshape(2, half_e, cap, q_cols)
        for d in range(1, n_e):
            to = e_at(d)
            send(
                dsend.at[a, to // half_e, lax.rem(to, half_e)],
                rows.at[a, x, e // half_e, lax.rem(e, half_e)],
                sd_sem.at[a, d],
                rd_sem.at[a, d],
                {"expert": to},
            )
        rows[a, x, e // half_e, lax.rem(e, half_e)] = dsend[a, e // half_e, lax.rem(e, half_e)]

    def dispatch_wait(a):
        for d in range(1, n_e):
            src = e_at(-d)
            arrive(
                rows.at[a, x, src // half_e, lax.rem(src, half_e)],
                sd_sem.at[a, d],
                rd_sem.at[a, d],
                {"expert": src},
            )

    right, left = x_at(1), x_at(-1)
    far = x_at(2)

    def gather_start(a):
        for h in range(2):
            send(rows.at[a, x, h], rows.at[a, x, h], sg_sem.at[a, 0, h], rg_sem.at[a, 0, h], {"tensor": right})
            g = 1 - h
            send(rows.at[a, x, g], rows.at[a, x, g], sg_sem.at[a, 1, g], rg_sem.at[a, 1, g], {"tensor": left})

    def gather_relay(a):
        arrive(rows.at[a, left, 0], sg_sem.at[a, 0, 0], rg_sem.at[a, 0, 0], {"tensor": left})
        send(rows.at[a, left, 0], rows.at[a, left, 0], sg_sem.at[a, 2, 0], rg_sem.at[a, 2, 0], {"tensor": right})
        arrive(rows.at[a, right, 1], sg_sem.at[a, 1, 1], rg_sem.at[a, 1, 1], {"tensor": right})
        send(rows.at[a, right, 1], rows.at[a, right, 1], sg_sem.at[a, 2, 1], rg_sem.at[a, 2, 1], {"tensor": left})

    def gather_near(a):
        arrive(rows.at[a, left, 1], sg_sem.at[a, 0, 1], rg_sem.at[a, 0, 1], {"tensor": left})
        arrive(rows.at[a, right, 0], sg_sem.at[a, 1, 0], rg_sem.at[a, 1, 0], {"tensor": right})

    def gather_far(a):
        arrive(rows.at[a, far, 0], sg_sem.at[a, 2, 0], rg_sem.at[a, 2, 0], {"tensor": left})
        arrive(rows.at[a, far, 1], sg_sem.at[a, 2, 1], rg_sem.at[a, 2, 1], {"tensor": right})

    def row_block(a, q):
        return rows[a, q].reshape(n_slots, q_cols)

    def put_part(b, q, value):
        part[b, q] = value.reshape(n_e, cap, q_cols).astype(BF16).reshape(2, half_e, cap, q_cols)

    def reduce_far(b):
        send(part.at[b, far, 0], rs_far.at[b, 0], sr_sem.at[b, 0], rr_sem.at[b, 0], {"tensor": right})
        send(part.at[b, far, 1], rs_far.at[b, 1], sr_sem.at[b, 1], rr_sem.at[b, 1], {"tensor": left})

    def reduce_near(b):
        send(part.at[b, right, 1], rs_near.at[b, 0, 1], sr_sem.at[b, 2], rr_sem.at[b, 2], {"tensor": right})
        send(part.at[b, left, 0], rs_near.at[b, 1, 0], sr_sem.at[b, 3], rr_sem.at[b, 3], {"tensor": left})

    def reduce_relay(b):
        arrive(rs_far.at[b, 0], sr_sem.at[b, 0], rr_sem.at[b, 0], {"tensor": left})
        rs_sum[b, 0] = (rs_far[b, 0].astype(F32) + part[b, right, 0].astype(F32)).astype(BF16)
        send(rs_sum.at[b, 0], rs_near.at[b, 0, 0], sr_sem.at[b, 4], rr_sem.at[b, 4], {"tensor": right})
        arrive(rs_far.at[b, 1], sr_sem.at[b, 1], rr_sem.at[b, 1], {"tensor": right})
        rs_sum[b, 1] = (rs_far[b, 1].astype(F32) + part[b, left, 1].astype(F32)).astype(BF16)
        send(rs_sum.at[b, 1], rs_near.at[b, 1, 1], sr_sem.at[b, 5], rr_sem.at[b, 5], {"tensor": left})

    def reduce_end(b):
        arrive(rs_near.at[b, 0, 1], sr_sem.at[b, 2], rr_sem.at[b, 2], {"tensor": left})
        arrive(rs_near.at[b, 1, 0], sr_sem.at[b, 3], rr_sem.at[b, 3], {"tensor": right})
        arrive(rs_near.at[b, 0, 0], sr_sem.at[b, 4], rr_sem.at[b, 4], {"tensor": left})
        arrive(rs_near.at[b, 1, 1], sr_sem.at[b, 5], rr_sem.at[b, 5], {"tensor": right})
        total = part[b, x].astype(F32) + rs_near[b, 0].astype(F32) + rs_near[b, 1].astype(F32)
        ysend[b] = total.astype(BF16)
        for d in range(1, n_e):
            to = e_at(d)
            send(
                ysend.at[b, to // half_e, lax.rem(to, half_e)],
                yret.at[b, e // half_e, lax.rem(e, half_e)],
                sy_sem.at[b, d],
                ry_sem.at[b, d],
                {"expert": to},
            )
        yret[b, e // half_e, lax.rem(e, half_e)] = ysend[b, e // half_e, lax.rem(e, half_e)]

    def combine(b):
        for d in range(1, n_e):
            src = e_at(-d)
            arrive(
                yret.at[b, src // half_e, lax.rem(src, half_e)],
                sy_sem.at[b, d],
                ry_sem.at[b, d],
                {"expert": src},
            )
        slots = yret[b].reshape(n_slots, q_cols)
        if b == 0:
            mixed = dot(weighted_back[0], slots) + dot(weighted_back[1], slots)
        else:
            mixed = dot(placed_back, slots)
        group[...] = mixed
        for j in range(n_x):
            csend[b, j] = group[pl.ds(j * tokens_here, tokens_here), :].astype(BF16)
        for d in range(1, n_x):
            to = x_at(d)
            send(csend.at[b, to], fin.at[b, x], sc_sem.at[b, d], rc_sem.at[b, d], {"tensor": to})
        fin[b, x] = csend[b, x]

    def finish(b, out_ref):
        for d in range(1, n_x):
            src = x_at(-d)
            arrive(fin.at[b, src], sc_sem.at[b, d], rc_sem.at[b, d], {"tensor": src})
        for j in range(n_x):
            out_ref[:, pl.ds(j * q_cols, q_cols)] = fin[b, j]

    z_up, z_down = z_at(1), z_at(-1)

    def z_send(way, s, i):
        send(
            zout.at[way, s, i],
            zin.at[way, s, i],
            sz_sem.at[way, s, i],
            rz_sem.at[way, s, i],
            {"dp": z_up if way == 0 else z_down},
        )

    def z_arrive(way, s, i):
        arrive(
            zin.at[way, s, i],
            sz_sem.at[way, s, i],
            rz_sem.at[way, s, i],
            {"dp": z_down if way == 0 else z_up},
        )
        return zin[way, s, i].astype(F32)

    def z_step(s):
        targets = (z_at(half_z - s), z_at(s - half_z))
        for j in range(SUB if s > 0 else SUB // 2):
            early = j < SUB // 2
            for way in range(2):
                i = j if way == 0 else SUB - 1 - j
                value = term[targets[way], i]
                if s > 1 or (s == 1 and early):
                    value = value + z_arrive(way, s - 1, i)
                zout[way, s, i] = value.astype(BF16)
                z_send(way, s, i)

    def z_finish():
        for i in range(SUB):
            total = term[z, i] + z_arrive(0, half_z - 1, i) + z_arrive(1, half_z - 1, i)
            term[z, i] = total * (1.0 / n_z)
        whole = term[z].reshape(hidden, term.shape[3])
        gd_ref[...] = whole.T.astype(BF16)

    dispatch(0)
    dispatch(1)
    dispatch_wait(0)
    gather_start(0)
    loads[0].wait()
    loads[1].wait()
    block = row_block(0, x)
    gate_s[...] = dot(block, gw[x])
    up_s[...] = dot(block, uw[x])
    dispatch_wait(1)
    gather_start(1)
    gather_relay(0)
    gather_near(0)
    for q in (left, right):
        block = row_block(0, q)
        gate_s[...] += dot(block, gw[q])
        up_s[...] += dot(block, uw[q])
    gather_far(0)
    block = row_block(0, far)
    gate = gate_s[...] + dot(block, gw[far])
    up = up_s[...] + dot(block, uw[far])
    squash = 1.0 / (1.0 + jnp.exp(-gate))
    swish = gate * squash
    act = swish * up
    gate_s[...] = up * squash * (1.0 + gate * (1.0 - squash))
    up_s[...] = swish
    act_b = act.astype(BF16)
    act_t = act.T.astype(BF16)
    loads[2].wait()
    gather_relay(1)
    put_part(0, far, dot_t(act_b, dw[far]))
    reduce_far(0)
    for q in (right, left):
        put_part(0, q, dot_t(act_b, dw[q]))
    reduce_near(0)
    put_part(0, x, dot_t(act_b, dw[x]))
    gather_near(1)
    gather_far(1)
    chunk_cols = term.shape[3]
    per_quarter = q_cols // chunk_cols
    for q in range(n_x):
        block = dot(act_t, row_block(1, q))
        for c in range(per_quarter):
            piece = block[:, c * chunk_cols : (c + 1) * chunk_cols]
            term[q * per_quarter + c] = piece.reshape(SUB, hidden // SUB, chunk_cols)
    z_step(0)
    reduce_relay(0)
    grad = None
    for q in range(n_x):
        piece = dot(row_block(1, q), dw[q])
        grad = piece if grad is None else grad + piece
    gate_back = (grad * gate_s[...]).astype(BF16)
    up_back = (grad * up_s[...]).astype(BF16)
    z_step(1)

    def input_part(q):
        put_part(1, q, dot_t(gate_back, gw[q]) + dot_t(up_back, uw[q]))

    input_part(far)
    reduce_far(1)
    input_part(right)
    input_part(left)
    reduce_near(1)
    reduce_end(0)
    z_step(2)
    input_part(x)
    reduce_relay(1)
    z_step(3)
    reduce_end(1)
    combine(0)
    z_step(4)
    z_step(5)
    combine(1)
    finish(0, lo_ref)
    z_step(6)
    finish(1, gt_ref)
    z_step(7)
    z_finish()
    for copy in started:
        copy.wait_send()


def shards(
    tokens, routes, positions, combine_weights, cotangent, gate_weight, up_weight, down_weight
):
    n_z, n_e, n_x = lax.axis_size("dp"), lax.axis_size("expert"), lax.axis_size("tensor")
    tokens_here, width = tokens.shape
    group_size = routes.shape[0]
    cap = group_size // 2
    hidden = gate_weight.shape[2]
    q_cols = width // n_x
    n_slots = n_e * cap
    half_e, half_z = n_e // 2, n_z // 2
    z_rows = width // n_z
    vmem = pl.BlockSpec(memory_space=pltpu.VMEM)
    hbm = pl.BlockSpec(memory_space=pl.ANY)
    dma = pltpu.SemaphoreType.DMA
    weights = [
        w.reshape(n_x, q_cols, hidden) for w in (gate_weight, up_weight, down_weight)
    ]
    quarter = (half_e, cap, q_cols)
    return pl.pallas_call(
        functools.partial(kernel, n_z, n_e),
        out_shape=(
            jax.ShapeDtypeStruct((tokens_here, width), BF16),
            jax.ShapeDtypeStruct((tokens_here, width), BF16),
            jax.ShapeDtypeStruct((z_rows, hidden), BF16),
        ),
        in_specs=[vmem] * 5 + [hbm] * 3,
        out_specs=(vmem, vmem, vmem),
        scratch_shapes=[pltpu.VMEM((n_x, q_cols, hidden), BF16)] * 3
        + [
            pltpu.VMEM((2, n_x, tokens_here, q_cols), BF16),
            pltpu.VMEM((group_size, q_cols), F32),
            pltpu.VMEM((2, 2) + quarter, BF16),
            pltpu.VMEM((2, n_x, 2) + quarter, BF16),
            pltpu.VMEM((n_slots, hidden), F32),
            pltpu.VMEM((n_slots, hidden), F32),
            pltpu.VMEM((2, n_x, 2) + quarter, BF16),
            pltpu.VMEM((2, 2) + quarter, BF16),
            pltpu.VMEM((2, 2) + quarter, BF16),
            pltpu.VMEM((2, 2, 2) + quarter, BF16),
            pltpu.VMEM((2, 2) + quarter, BF16),
            pltpu.VMEM((2, 2) + quarter, BF16),
            pltpu.VMEM((2, n_x, tokens_here, q_cols), BF16),
            pltpu.VMEM((2, n_x, tokens_here, q_cols), BF16),
            pltpu.VMEM((n_z, SUB, hidden // SUB, z_rows), F32),
            pltpu.VMEM((2, half_z, SUB, hidden // SUB, z_rows), BF16),
            pltpu.VMEM((2, half_z, SUB, hidden // SUB, z_rows), BF16),
            dma((3,)),
            dma((2, n_x)),
            dma((2, n_x)),
            dma((2, n_e)),
            dma((2, n_e)),
            dma((2, 3, 2)),
            dma((2, 3, 2)),
            dma((2, 6)),
            dma((2, 6)),
            dma((2, n_e)),
            dma((2, n_e)),
            dma((2, n_x)),
            dma((2, n_x)),
            dma((2, half_z, SUB)),
            dma((2, half_z, SUB)),
        ],
        compiler_params=pltpu.CompilerParams(
            collective_id=0, has_side_effects=True, vmem_limit_bytes=56 * 1024 * 1024
        ),
    )(tokens, cotangent, routes, positions, combine_weights, *weights)


def body(*arrays):
    layer_out, grad_tokens, grad_down = shards(*arrays)
    return layer_out, grad_tokens, grad_down[None]


def solution(mesh):
    return jax.shard_map(
        body,
        mesh=mesh,
        in_specs=(
            P(("dp", "expert", "tensor"), None),
            P(("dp", "expert"), None),
            P(("dp", "expert"), None),
            P(("dp", "expert"), None),
            P(("dp", "expert", "tensor"), None),
            P("expert", None, "tensor"),
            P("expert", None, "tensor"),
            P("expert", None, "tensor"),
        ),
        out_specs=(
            P(("dp", "expert", "tensor"), None),
            P(("dp", "expert", "tensor"), None),
            P("expert", "dp", "tensor"),
        ),
        check_vma=False,
    )
```

```python
import functools

import jax
import jax.numpy as jnp
from jax import lax
from jax.experimental import pallas as pl
from jax.experimental.pallas import tpu as pltpu
from jax.sharding import PartitionSpec as P

MESH = pl.DeviceIdType.MESH
F32 = jnp.float32
BF16 = jnp.bfloat16
SUB = 4


def dot(left, right):
    return lax.dot_general(left, right, (((1,), (0,)), ((), ())), preferred_element_type=F32)


def dot_t(left, right):
    return lax.dot_general(left, right, (((1,), (1,)), ((), ())), preferred_element_type=F32)


def kernel(
    n_z,
    n_e,
    tok_ref,
    cot_ref,
    routes_ref,
    pos_ref,
    cw_ref,
    gw_hbm,
    uw_hbm,
    dw_hbm,
    lo_ref,
    gt_ref,
    gd_ref,
    gw,
    uw,
    dw,
    xin,
    group,
    dsend,
    rows,
    gate_s,
    up_s,
    part,
    rs_far,
    rs_sum,
    rs_near,
    ysend,
    yret,
    csend,
    fin,
    term,
    zin,
    zout,
    w_sem,
    sx_sem,
    rx_sem,
    sd_sem,
    rd_sem,
    sg_sem,
    rg_sem,
    sr_sem,
    rr_sem,
    sy_sem,
    ry_sem,
    sc_sem,
    rc_sem,
    sz_sem,
    rz_sem,
):
    n_x, _, _, cap, q_cols = rows.shape[1:]
    tokens_here = tok_ref.shape[0]
    group_size = routes_ref.shape[1]
    n_slots = n_e * cap
    half_e = n_e // 2
    half_z = n_z // 2
    hidden = gate_s.shape[1]
    x = lax.axis_index("tensor")
    e = lax.axis_index("expert")
    z = lax.axis_index("dp")

    def x_at(d):
        return lax.rem(x + d + n_x, n_x)

    def e_at(d):
        return lax.rem(e + d + n_e, n_e)

    def z_at(d):
        return lax.rem(z + d + 2 * n_z, n_z)

    started = []

    def send(src, dst, send_sem, recv_sem, device):
        copy = pltpu.make_async_remote_copy(
            src_ref=src,
            dst_ref=dst,
            send_sem=send_sem,
            recv_sem=recv_sem,
            device_id=device,
            device_id_type=MESH,
        )
        copy.start()
        started.append(copy)

    def arrive(dst, send_sem, recv_sem, device):
        pltpu.make_async_remote_copy(
            src_ref=dst,
            dst_ref=dst,
            send_sem=send_sem,
            recv_sem=recv_sem,
            device_id=device,
            device_id_type=MESH,
        ).wait_recv()

    loads = []
    for i, (src, dst) in enumerate(((gw_hbm, gw), (uw_hbm, uw), (dw_hbm, dw))):
        load = pltpu.make_async_copy(src, dst, w_sem.at[i])
        load.start()
        loads.append(load)

    barrier = pltpu.get_barrier_semaphore()
    for d in range(1, n_x):
        pl.semaphore_signal(barrier, inc=1, device_id={"tensor": x_at(d)}, device_id_type=MESH)
    for d in range(1, n_e):
        pl.semaphore_signal(barrier, inc=1, device_id={"expert": e_at(d)}, device_id_type=MESH)
    for d in (1, -1):
        pl.semaphore_signal(barrier, inc=1, device_id={"dp": z_at(d)}, device_id_type=MESH)
    pl.semaphore_wait(barrier, n_x - 1 + n_e - 1 + 2)

    sources = (tok_ref, cot_ref)

    def quarter_of(a, q):
        return sources[a].at[:, pl.ds(pl.multiple_of(q * q_cols, q_cols), q_cols)]

    for a in range(2):
        for d in range(1, n_x):
            q = x_at(d)
            send(
                quarter_of(a, q),
                xin.at[a, x],
                sx_sem.at[a, d],
                rx_sem.at[a, d],
                {"tensor": q},
            )
    for a in range(2):
        xin[a, x] = quarter_of(a, x)[...]

    slot_ids = routes_ref[...] * cap + pos_ref[...]
    gains = cw_ref[...]
    numbers = lax.broadcasted_iota(jnp.int32, (n_slots, group_size), 0)
    placed = jnp.zeros((n_slots, group_size), F32)
    weighted = jnp.zeros((n_slots, group_size), F32)
    for k in range(slot_ids.shape[0]):
        match = numbers == slot_ids[k : k + 1, :]
        placed = placed + jnp.where(match, 1.0, 0.0)
        weighted = weighted + jnp.where(match, gains[k : k + 1, :], 0.0)

    def pieces(table):
        high = table.astype(BF16)
        return high, (table - high.astype(F32)).astype(BF16)

    placed_in = placed.astype(BF16)
    weighted_in = pieces(weighted)
    placed_back = placed.T.astype(BF16)
    weighted_back = pieces(weighted.T)

    def dispatch(a):
        for d in range(1, n_x):
            src = x_at(-d)
            arrive(xin.at[a, src], sx_sem.at[a, d], rx_sem.at[a, d], {"tensor": src})
        for j in range(n_x):
            group[pl.ds(j * tokens_here, tokens_here), :] = xin[a, j].astype(F32)
        here = group[...].astype(BF16)
        if a == 0:
            slots = dot(placed_in, here)
        else:
            slots = dot(weighted_in[0], here) + dot(weighted_in[1], here)
        dsend[a] = slots.reshape(n_e, cap, q_cols).astype(BF16).reshape(2, half_e, cap, q_cols)
        for d in range(1, n_e):
            to = e_at(d)
            send(
                dsend.at[a, to // half_e, lax.rem(to, half_e)],
                rows.at[a, x, e // half_e, lax.rem(e, half_e)],
                sd_sem.at[a, d],
                rd_sem.at[a, d],
                {"expert": to},
            )
        rows[a, x, e // half_e, lax.rem(e, half_e)] = dsend[a, e // half_e, lax.rem(e, half_e)]

    def dispatch_wait(a):
        for d in range(1, n_e):
            src = e_at(-d)
            arrive(
                rows.at[a, x, src // half_e, lax.rem(src, half_e)],
                sd_sem.at[a, d],
                rd_sem.at[a, d],
                {"expert": src},
            )

    right, left = x_at(1), x_at(-1)
    far = x_at(2)

    def gather_start(a):
        for h in range(2):
            send(rows.at[a, x, h], rows.at[a, x, h], sg_sem.at[a, 0, h], rg_sem.at[a, 0, h], {"tensor": right})
            g = 1 - h
            send(rows.at[a, x, g], rows.at[a, x, g], sg_sem.at[a, 1, g], rg_sem.at[a, 1, g], {"tensor": left})

    def gather_relay(a):
        arrive(rows.at[a, left, 0], sg_sem.at[a, 0, 0], rg_sem.at[a, 0, 0], {"tensor": left})
        send(rows.at[a, left, 0], rows.at[a, left, 0], sg_sem.at[a, 2, 0], rg_sem.at[a, 2, 0], {"tensor": right})
        arrive(rows.at[a, right, 1], sg_sem.at[a, 1, 1], rg_sem.at[a, 1, 1], {"tensor": right})
        send(rows.at[a, right, 1], rows.at[a, right, 1], sg_sem.at[a, 2, 1], rg_sem.at[a, 2, 1], {"tensor": left})

    def gather_near(a):
        arrive(rows.at[a, left, 1], sg_sem.at[a, 0, 1], rg_sem.at[a, 0, 1], {"tensor": left})
        arrive(rows.at[a, right, 0], sg_sem.at[a, 1, 0], rg_sem.at[a, 1, 0], {"tensor": right})

    def gather_far(a):
        arrive(rows.at[a, far, 0], sg_sem.at[a, 2, 0], rg_sem.at[a, 2, 0], {"tensor": left})
        arrive(rows.at[a, far, 1], sg_sem.at[a, 2, 1], rg_sem.at[a, 2, 1], {"tensor": right})

    def weight(ref, q):
        return ref[:, pl.ds(pl.multiple_of(q * q_cols, q_cols), q_cols)]

    def row_block(a, q):
        return rows[a, q].reshape(n_slots, q_cols)

    def put_part(b, q, value):
        part[b, q] = value.reshape(n_e, cap, q_cols).astype(BF16).reshape(2, half_e, cap, q_cols)

    def reduce_far(b):
        send(part.at[b, far, 0], rs_far.at[b, 0], sr_sem.at[b, 0], rr_sem.at[b, 0], {"tensor": right})
        send(part.at[b, far, 1], rs_far.at[b, 1], sr_sem.at[b, 1], rr_sem.at[b, 1], {"tensor": left})

    def reduce_near(b):
        send(part.at[b, right, 1], rs_near.at[b, 0, 1], sr_sem.at[b, 2], rr_sem.at[b, 2], {"tensor": right})
        send(part.at[b, left, 0], rs_near.at[b, 1, 0], sr_sem.at[b, 3], rr_sem.at[b, 3], {"tensor": left})

    def reduce_relay(b):
        arrive(rs_far.at[b, 0], sr_sem.at[b, 0], rr_sem.at[b, 0], {"tensor": left})
        rs_sum[b, 0] = (rs_far[b, 0].astype(F32) + part[b, right, 0].astype(F32)).astype(BF16)
        send(rs_sum.at[b, 0], rs_near.at[b, 0, 0], sr_sem.at[b, 4], rr_sem.at[b, 4], {"tensor": right})
        arrive(rs_far.at[b, 1], sr_sem.at[b, 1], rr_sem.at[b, 1], {"tensor": right})
        rs_sum[b, 1] = (rs_far[b, 1].astype(F32) + part[b, left, 1].astype(F32)).astype(BF16)
        send(rs_sum.at[b, 1], rs_near.at[b, 1, 1], sr_sem.at[b, 5], rr_sem.at[b, 5], {"tensor": left})

    def reduce_end(b):
        arrive(rs_near.at[b, 0, 1], sr_sem.at[b, 2], rr_sem.at[b, 2], {"tensor": left})
        arrive(rs_near.at[b, 1, 0], sr_sem.at[b, 3], rr_sem.at[b, 3], {"tensor": right})
        arrive(rs_near.at[b, 0, 0], sr_sem.at[b, 4], rr_sem.at[b, 4], {"tensor": left})
        arrive(rs_near.at[b, 1, 1], sr_sem.at[b, 5], rr_sem.at[b, 5], {"tensor": right})
        total = part[b, x].astype(F32) + rs_near[b, 0].astype(F32) + rs_near[b, 1].astype(F32)
        ysend[b] = total.astype(BF16)
        for d in range(1, n_e):
            to = e_at(d)
            send(
                ysend.at[b, to // half_e, lax.rem(to, half_e)],
                yret.at[b, e // half_e, lax.rem(e, half_e)],
                sy_sem.at[b, d],
                ry_sem.at[b, d],
                {"expert": to},
            )
        yret[b, e // half_e, lax.rem(e, half_e)] = ysend[b, e // half_e, lax.rem(e, half_e)]

    def combine(b):
        for d in range(1, n_e):
            src = e_at(-d)
            arrive(
                yret.at[b, src // half_e, lax.rem(src, half_e)],
                sy_sem.at[b, d],
                ry_sem.at[b, d],
                {"expert": src},
            )
        slots = yret[b].reshape(n_slots, q_cols)
        if b == 0:
            mixed = dot(weighted_back[0], slots) + dot(weighted_back[1], slots)
        else:
            mixed = dot(placed_back, slots)
        group[...] = mixed
        for j in range(n_x):
            csend[b, j] = group[pl.ds(j * tokens_here, tokens_here), :].astype(BF16)
        for d in range(1, n_x):
            to = x_at(d)
            send(csend.at[b, to], fin.at[b, x], sc_sem.at[b, d], rc_sem.at[b, d], {"tensor": to})
        fin[b, x] = csend[b, x]

    def finish(b, out_ref):
        for d in range(1, n_x):
            src = x_at(-d)
            arrive(fin.at[b, src], sc_sem.at[b, d], rc_sem.at[b, d], {"tensor": src})
        for j in range(n_x):
            out_ref[:, pl.ds(j * q_cols, q_cols)] = fin[b, j]

    z_up, z_down = z_at(1), z_at(-1)

    def z_send(way, s, i):
        send(
            zout.at[way, s, i],
            zin.at[way, s, i],
            sz_sem.at[way, s, i],
            rz_sem.at[way, s, i],
            {"dp": z_up if way == 0 else z_down},
        )

    def z_arrive(way, s, i):
        arrive(
            zin.at[way, s, i],
            sz_sem.at[way, s, i],
            rz_sem.at[way, s, i],
            {"dp": z_down if way == 0 else z_up},
        )
        return zin[way, s, i].astype(F32)

    def z_step(s):
        targets = (z_at(half_z - s), z_at(s - half_z))
        for j in range(SUB if s > 0 else SUB // 2):
            early = j < SUB // 2
            for way in range(2):
                i = j if way == 0 else SUB - 1 - j
                value = term[targets[way], i]
                if s > 1 or (s == 1 and early):
                    value = value + z_arrive(way, s - 1, i)
                zout[way, s, i] = value.astype(BF16)
                z_send(way, s, i)

    def z_finish():
        for i in range(SUB):
            total = term[z, i] + z_arrive(0, half_z - 1, i) + z_arrive(1, half_z - 1, i)
            rows_here = hidden // SUB
            gd_ref[pl.ds(i * rows_here, rows_here), :] = (total * (1.0 / n_z)).astype(BF16)

    dispatch(0)
    dispatch(1)
    dispatch_wait(0)
    gather_start(0)
    loads[0].wait()
    loads[1].wait()
    block = row_block(0, x)
    gate_s[...] = dot_t(block, weight(gw, x))
    up_s[...] = dot_t(block, weight(uw, x))
    dispatch_wait(1)
    gather_start(1)
    gather_relay(0)
    gather_near(0)
    for q in (left, right):
        block = row_block(0, q)
        gate_s[...] += dot_t(block, weight(gw, q))
        up_s[...] += dot_t(block, weight(uw, q))
    gather_far(0)
    block = row_block(0, far)
    gate = gate_s[...] + dot_t(block, weight(gw, far))
    up = up_s[...] + dot_t(block, weight(uw, far))
    squash = 1.0 / (1.0 + jnp.exp(-gate))
    swish = gate * squash
    act = swish * up
    gate_s[...] = up * squash * (1.0 + gate * (1.0 - squash))
    up_s[...] = swish
    act_b = act.astype(BF16)
    act_t = act.T.astype(BF16)
    loads[2].wait()
    gather_relay(1)
    put_part(0, far, dot(act_b, weight(dw, far)))
    reduce_far(0)
    for q in (right, left):
        put_part(0, q, dot(act_b, weight(dw, q)))
    reduce_near(0)
    put_part(0, x, dot(act_b, weight(dw, x)))
    gather_near(1)
    gather_far(1)
    chunk_cols = term.shape[3]
    per_quarter = q_cols // chunk_cols
    for q in range(n_x):
        block = dot(act_t, row_block(1, q))
        for c in range(per_quarter):
            piece = block[:, c * chunk_cols : (c + 1) * chunk_cols]
            term[q * per_quarter + c] = piece.reshape(SUB, hidden // SUB, chunk_cols)
    z_step(0)
    reduce_relay(0)
    grad = None
    for q in range(n_x):
        piece = dot_t(row_block(1, q), weight(dw, q))
        grad = piece if grad is None else grad + piece
    gate_back = (grad * gate_s[...]).astype(BF16)
    up_back = (grad * up_s[...]).astype(BF16)
    z_step(1)

    def input_part(q):
        put_part(1, q, dot(gate_back, weight(gw, q)) + dot(up_back, weight(uw, q)))

    input_part(far)
    reduce_far(1)
    input_part(right)
    input_part(left)
    reduce_near(1)
    reduce_end(0)
    z_step(2)
    input_part(x)
    reduce_relay(1)
    z_step(3)
    reduce_end(1)
    combine(0)
    z_step(4)
    z_step(5)
    combine(1)
    finish(0, lo_ref)
    z_step(6)
    finish(1, gt_ref)
    z_step(7)
    z_finish()
    for copy in started:
        copy.wait_send()


def shards(
    tokens, routes, positions, combine_weights, cotangent, gate_weight, up_weight, down_weight
):
    n_z, n_e, n_x = lax.axis_size("dp"), lax.axis_size("expert"), lax.axis_size("tensor")
    tokens_here, width = tokens.shape
    group_size = routes.shape[0]
    cap = group_size // 2
    hidden = gate_weight.shape[2]
    q_cols = width // n_x
    n_slots = n_e * cap
    half_e, half_z = n_e // 2, n_z // 2
    z_rows = width // n_z
    vmem = pl.BlockSpec(memory_space=pltpu.VMEM)
    hbm = pl.BlockSpec(memory_space=pl.ANY)
    dma = pltpu.SemaphoreType.DMA
    weights = [jnp.swapaxes(w[0], 0, 1) for w in (gate_weight, up_weight, down_weight)]
    plans = [v.T for v in (routes, positions, combine_weights)]
    quarter = (half_e, cap, q_cols)
    return pl.pallas_call(
        functools.partial(kernel, n_z, n_e),
        out_shape=(
            jax.ShapeDtypeStruct((tokens_here, width), BF16),
            jax.ShapeDtypeStruct((tokens_here, width), BF16),
            jax.ShapeDtypeStruct((hidden, z_rows), BF16),
        ),
        in_specs=[vmem] * 5 + [hbm] * 3,
        out_specs=(vmem, vmem, vmem),
        scratch_shapes=[pltpu.VMEM((hidden, width), BF16)] * 3
        + [
            pltpu.VMEM((2, n_x, tokens_here, q_cols), BF16),
            pltpu.VMEM((group_size, q_cols), F32),
            pltpu.VMEM((2, 2) + quarter, BF16),
            pltpu.VMEM((2, n_x, 2) + quarter, BF16),
            pltpu.VMEM((n_slots, hidden), F32),
            pltpu.VMEM((n_slots, hidden), F32),
            pltpu.VMEM((2, n_x, 2) + quarter, BF16),
            pltpu.VMEM((2, 2) + quarter, BF16),
            pltpu.VMEM((2, 2) + quarter, BF16),
            pltpu.VMEM((2, 2, 2) + quarter, BF16),
            pltpu.VMEM((2, 2) + quarter, BF16),
            pltpu.VMEM((2, 2) + quarter, BF16),
            pltpu.VMEM((2, n_x, tokens_here, q_cols), BF16),
            pltpu.VMEM((2, n_x, tokens_here, q_cols), BF16),
            pltpu.VMEM((n_z, SUB, hidden // SUB, z_rows), F32),
            pltpu.VMEM((2, half_z, SUB, hidden // SUB, z_rows), BF16),
            pltpu.VMEM((2, half_z, SUB, hidden // SUB, z_rows), BF16),
            dma((3,)),
            dma((2, n_x)),
            dma((2, n_x)),
            dma((2, n_e)),
            dma((2, n_e)),
            dma((2, 3, 2)),
            dma((2, 3, 2)),
            dma((2, 6)),
            dma((2, 6)),
            dma((2, n_e)),
            dma((2, n_e)),
            dma((2, n_x)),
            dma((2, n_x)),
            dma((2, half_z, SUB)),
            dma((2, half_z, SUB)),
        ],
        compiler_params=pltpu.CompilerParams(
            collective_id=0, has_side_effects=True, vmem_limit_bytes=56 * 1024 * 1024
        ),
    )(tokens, cotangent, *plans, *weights)


def place(*refs):
    half = len(refs) // 2
    for source, target in zip(refs[:half], refs[half:]):
        target[...] = source[...]


def body(*arrays):
    results = shards(*arrays)
    layer_out, grad_tokens, grad_down = pl.pallas_call(
        place,
        out_shape=tuple(jax.ShapeDtypeStruct(r.shape, r.dtype) for r in results),
        in_specs=[pl.BlockSpec(memory_space=pltpu.VMEM)] * 3,
        out_specs=(pl.BlockSpec(memory_space=pltpu.VMEM),) * 3,
    )(*results)
    return layer_out, grad_tokens, jnp.swapaxes(grad_down, 0, 1)[None]


def solution(mesh):
    return jax.shard_map(
        body,
        mesh=mesh,
        in_specs=(
            P(("dp", "expert", "tensor"), None),
            P(("dp", "expert"), None),
            P(("dp", "expert"), None),
            P(("dp", "expert"), None),
            P(("dp", "expert", "tensor"), None),
            P("expert", None, "tensor"),
            P("expert", None, "tensor"),
            P("expert", None, "tensor"),
        ),
        out_specs=(
            P(("dp", "expert", "tensor"), None),
            P(("dp", "expert", "tensor"), None),
            P("expert", "dp", "tensor"),
        ),
        check_vma=False,
    )
```

```python
import functools

import jax
import jax.numpy as jnp
from jax import lax
from jax.experimental import pallas as pl
from jax.experimental.pallas import tpu as pltpu
from jax.sharding import PartitionSpec as P

MESH = pl.DeviceIdType.MESH
F32 = jnp.float32
BF16 = jnp.bfloat16
SUB = 4


def dot(left, right):
    return lax.dot_general(left, right, (((1,), (0,)), ((), ())), preferred_element_type=F32)


def dot_t(left, right):
    return lax.dot_general(left, right, (((1,), (1,)), ((), ())), preferred_element_type=F32)


def kernel(
    n_z,
    n_e,
    tok_hbm,
    cot_hbm,
    routes_hbm,
    pos_hbm,
    cw_hbm,
    gw_hbm,
    uw_hbm,
    dw_hbm,
    lo_hbm,
    gt_hbm,
    gd_hbm,
    tok_ref,
    cot_ref,
    routes_ref,
    pos_ref,
    cw_ref,
    gw,
    uw,
    dw,
    xin,
    group,
    dsend,
    rows,
    gate_s,
    up_s,
    part,
    rs_far,
    rs_sum,
    rs_near,
    ysend,
    yret,
    csend,
    acts,
    pair,
    term,
    zin,
    zout,
    gd_out,
    in_sem,
    out_sem,
    w_sem,
    sx_sem,
    rx_sem,
    sd_sem,
    rd_sem,
    sg_sem,
    rg_sem,
    sr_sem,
    rr_sem,
    sy_sem,
    ry_sem,
    sc_sem,
    rc_sem,
    sa_sem,
    ra_sem,
    sp_sem,
    rp_sem,
    sz_sem,
    rz_sem,
):
    n_x, _, _, cap, q_cols = rows.shape[1:]
    tokens_here = tok_ref.shape[0]
    group_size = routes_ref.shape[1]
    n_slots = n_e * cap
    half_e = n_e // 2
    n_pairs = n_z // 2
    half_z = n_pairs // 2
    hidden = gate_s.shape[1]
    x = lax.axis_index("tensor")
    e = lax.axis_index("expert")
    z = lax.axis_index("dp")

    def x_at(d):
        return lax.rem(x + d + n_x, n_x)

    def e_at(d):
        return lax.rem(e + d + n_e, n_e)

    def z_at(d):
        return lax.rem(z + d + 2 * n_z, n_z)

    started = []

    def send(src, dst, send_sem, recv_sem, device):
        copy = pltpu.make_async_remote_copy(
            src_ref=src,
            dst_ref=dst,
            send_sem=send_sem,
            recv_sem=recv_sem,
            device_id=device,
            device_id_type=MESH,
        )
        copy.start()
        started.append(copy)

    def arrive(dst, send_sem, recv_sem, device):
        pltpu.make_async_remote_copy(
            src_ref=dst,
            dst_ref=dst,
            send_sem=send_sem,
            recv_sem=recv_sem,
            device_id=device,
            device_id_type=MESH,
        ).wait_recv()

    fetches = []
    for i, (src, dst) in enumerate(
        (
            (routes_hbm, routes_ref),
            (pos_hbm, pos_ref),
            (cw_hbm, cw_ref),
            (tok_hbm, tok_ref),
            (cot_hbm, cot_ref),
        )
    ):
        fetch = pltpu.make_async_copy(src, dst, in_sem.at[i])
        fetch.start()
        fetches.append(fetch)
    barrier = pltpu.get_barrier_semaphore()
    for d in range(1, n_x):
        pl.semaphore_signal(barrier, inc=1, device_id={"tensor": x_at(d)}, device_id_type=MESH)
    for d in range(1, n_e):
        pl.semaphore_signal(barrier, inc=1, device_id={"expert": e_at(d)}, device_id_type=MESH)
    z_side = lax.rem(z, 2)
    partner = z + 1 - 2 * z_side
    z_up, z_down = z_at(2), z_at(-2)
    for to in (partner, z_up, z_down):
        pl.semaphore_signal(barrier, inc=1, device_id={"dp": to}, device_id_type=MESH)
    loads = []
    for i, (src, dst) in enumerate(((gw_hbm, gw), (uw_hbm, uw), (dw_hbm, dw))):
        load = pltpu.make_async_copy(src, dst, w_sem.at[i])
        load.start()
        loads.append(load)

    for fetch in fetches:
        fetch.wait()
    pl.semaphore_wait(barrier, n_x - 1 + n_e - 1 + 3)

    sources = (tok_ref, cot_ref)

    def quarter_of(a, q):
        return sources[a].at[:, pl.ds(pl.multiple_of(q * q_cols, q_cols), q_cols)]

    for a in range(2):
        for d in range(1, n_x):
            q = x_at(d)
            send(
                quarter_of(a, q),
                xin.at[a, x],
                sx_sem.at[a, d],
                rx_sem.at[a, d],
                {"tensor": q},
            )
    for a in range(2):
        xin[a, x] = quarter_of(a, x)[...]

    slot_ids = routes_ref[...] * cap + pos_ref[...]
    gains = cw_ref[...]
    numbers = lax.broadcasted_iota(jnp.int32, (n_slots, group_size), 0)
    placed = jnp.zeros((n_slots, group_size), F32)
    weighted = jnp.zeros((n_slots, group_size), F32)
    for k in range(slot_ids.shape[0]):
        match = numbers == slot_ids[k : k + 1, :]
        placed = placed + jnp.where(match, 1.0, 0.0)
        weighted = weighted + jnp.where(match, gains[k : k + 1, :], 0.0)

    def pieces(table):
        high = table.astype(BF16)
        return high, (table - high.astype(F32)).astype(BF16)

    placed_in = placed.astype(BF16)
    weighted_in = pieces(weighted)
    placed_back = placed.T.astype(BF16)
    weighted_back = pieces(weighted.T)

    def dispatch(a):
        for d in range(1, n_x):
            src = x_at(-d)
            arrive(xin.at[a, src], sx_sem.at[a, d], rx_sem.at[a, d], {"tensor": src})
        for j in range(n_x):
            group[pl.ds(j * tokens_here, tokens_here), :] = xin[a, j].astype(F32)
        here = group[...].astype(BF16)
        if a == 0:
            slots = dot(placed_in, here)
        else:
            slots = dot(weighted_in[0], here) + dot(weighted_in[1], here)
        dsend[a] = slots.reshape(n_e, cap, q_cols).astype(BF16).reshape(2, half_e, cap, q_cols)
        for d in range(1, n_e):
            to = e_at(d)
            send(
                dsend.at[a, to // half_e, lax.rem(to, half_e)],
                rows.at[a, x, e // half_e, lax.rem(e, half_e)],
                sd_sem.at[a, d],
                rd_sem.at[a, d],
                {"expert": to},
            )
        rows[a, x, e // half_e, lax.rem(e, half_e)] = dsend[a, e // half_e, lax.rem(e, half_e)]

    def dispatch_wait(a):
        for d in range(1, n_e):
            src = e_at(-d)
            arrive(
                rows.at[a, x, src // half_e, lax.rem(src, half_e)],
                sd_sem.at[a, d],
                rd_sem.at[a, d],
                {"expert": src},
            )

    right, left = x_at(1), x_at(-1)
    far = x_at(2)

    def gather_start(a, h):
        g = 1 - h
        send(rows.at[a, x, h], rows.at[a, x, h], sg_sem.at[a, 0, h], rg_sem.at[a, 0, h], {"tensor": right})
        send(rows.at[a, x, g], rows.at[a, x, g], sg_sem.at[a, 1, g], rg_sem.at[a, 1, g], {"tensor": left})

    def gather_relay(a):
        arrive(rows.at[a, left, 0], sg_sem.at[a, 0, 0], rg_sem.at[a, 0, 0], {"tensor": left})
        send(rows.at[a, left, 0], rows.at[a, left, 0], sg_sem.at[a, 2, 0], rg_sem.at[a, 2, 0], {"tensor": right})
        arrive(rows.at[a, right, 1], sg_sem.at[a, 1, 1], rg_sem.at[a, 1, 1], {"tensor": right})
        send(rows.at[a, right, 1], rows.at[a, right, 1], sg_sem.at[a, 2, 1], rg_sem.at[a, 2, 1], {"tensor": left})

    def gather_near(a):
        arrive(rows.at[a, left, 1], sg_sem.at[a, 0, 1], rg_sem.at[a, 0, 1], {"tensor": left})
        arrive(rows.at[a, right, 0], sg_sem.at[a, 1, 0], rg_sem.at[a, 1, 0], {"tensor": right})

    def gather_far(a):
        arrive(rows.at[a, far, 0], sg_sem.at[a, 2, 0], rg_sem.at[a, 2, 0], {"tensor": left})
        arrive(rows.at[a, far, 1], sg_sem.at[a, 2, 1], rg_sem.at[a, 2, 1], {"tensor": right})

    def weight(ref, q):
        return ref[:, pl.ds(pl.multiple_of(q * q_cols, q_cols), q_cols)]

    def row_block(a, q):
        return rows[a, q].reshape(n_slots, q_cols)

    def put_part(b, q, value):
        part[b, q] = value.reshape(n_e, cap, q_cols).astype(BF16).reshape(2, half_e, cap, q_cols)

    def reduce_far(b):
        send(part.at[b, far, 0], rs_far.at[b, 0], sr_sem.at[b, 0], rr_sem.at[b, 0], {"tensor": right})
        send(part.at[b, far, 1], rs_far.at[b, 1], sr_sem.at[b, 1], rr_sem.at[b, 1], {"tensor": left})

    def reduce_near(b):
        send(part.at[b, right, 1], rs_near.at[b, 0, 1], sr_sem.at[b, 2], rr_sem.at[b, 2], {"tensor": right})
        send(part.at[b, left, 0], rs_near.at[b, 1, 0], sr_sem.at[b, 3], rr_sem.at[b, 3], {"tensor": left})

    def reduce_relay(b):
        arrive(rs_far.at[b, 0], sr_sem.at[b, 0], rr_sem.at[b, 0], {"tensor": left})
        rs_sum[b, 0] = (rs_far[b, 0].astype(F32) + part[b, right, 0].astype(F32)).astype(BF16)
        send(rs_sum.at[b, 0], rs_near.at[b, 0, 0], sr_sem.at[b, 4], rr_sem.at[b, 4], {"tensor": right})
        arrive(rs_far.at[b, 1], sr_sem.at[b, 1], rr_sem.at[b, 1], {"tensor": right})
        rs_sum[b, 1] = (rs_far[b, 1].astype(F32) + part[b, left, 1].astype(F32)).astype(BF16)
        send(rs_sum.at[b, 1], rs_near.at[b, 1, 1], sr_sem.at[b, 5], rr_sem.at[b, 5], {"tensor": left})

    def reduce_end(b):
        arrive(rs_near.at[b, 0, 1], sr_sem.at[b, 2], rr_sem.at[b, 2], {"tensor": left})
        arrive(rs_near.at[b, 1, 0], sr_sem.at[b, 3], rr_sem.at[b, 3], {"tensor": right})
        arrive(rs_near.at[b, 0, 0], sr_sem.at[b, 4], rr_sem.at[b, 4], {"tensor": left})
        arrive(rs_near.at[b, 1, 1], sr_sem.at[b, 5], rr_sem.at[b, 5], {"tensor": right})
        total = part[b, x].astype(F32) + rs_near[b, 0].astype(F32) + rs_near[b, 1].astype(F32)
        ysend[b] = total.astype(BF16)
        for d in range(1, n_e):
            to = e_at(d)
            send(
                ysend.at[b, to // half_e, lax.rem(to, half_e)],
                yret.at[b, e // half_e, lax.rem(e, half_e)],
                sy_sem.at[b, d],
                ry_sem.at[b, d],
                {"expert": to},
            )
        yret[b, e // half_e, lax.rem(e, half_e)] = ysend[b, e // half_e, lax.rem(e, half_e)]

    stores = []
    results = (lo_hbm, gt_hbm)

    def result_of(b, q):
        return results[b].at[:, pl.ds(pl.multiple_of(q * q_cols, q_cols), q_cols)]

    def combine(b):
        for d in range(1, n_e):
            src = e_at(-d)
            arrive(
                yret.at[b, src // half_e, lax.rem(src, half_e)],
                sy_sem.at[b, d],
                ry_sem.at[b, d],
                {"expert": src},
            )
        slots = yret[b].reshape(n_slots, q_cols)
        if b == 0:
            mixed = dot(weighted_back[0], slots) + dot(weighted_back[1], slots)
        else:
            mixed = dot(placed_back, slots)
        group[...] = mixed
        for j in range(n_x):
            csend[b, j] = group[pl.ds(j * tokens_here, tokens_here), :].astype(BF16)
        for d in range(1, n_x):
            to = x_at(d)
            send(csend.at[b, to], result_of(b, x), sc_sem.at[b, d], rc_sem.at[b, d], {"tensor": to})
        own = pltpu.make_async_copy(csend.at[b, x], result_of(b, x), out_sem.at[b])
        own.start()
        stores.append(own)

    def finish(b):
        for d in range(1, n_x):
            src = x_at(-d)
            arrive(result_of(b, src), sc_sem.at[b, d], rc_sem.at[b, d], {"tensor": src})

    chunk_cols = term.shape[3]
    pair_chunks = q_cols // chunk_cols // 2

    def act_send():
        send(acts.at[0], acts.at[1], sa_sem.at[0], ra_sem.at[0], {"dp": partner})

    def act_arrive():
        arrive(acts.at[1], sa_sem.at[0], ra_sem.at[0], {"dp": partner})

    def columns(q, m, side):
        start = pl.multiple_of((2 * m + side) * chunk_cols, chunk_cols)
        return rows.at[1, q, :, :, :, pl.ds(start, chunk_cols)]

    def pair_send(q):
        for m in range(pair_chunks):
            send(
                columns(q, m, 1 - z_side),
                pair.at[q, m],
                sp_sem.at[q, m],
                rp_sem.at[q, m],
                {"dp": partner},
            )

    def pair_arrive(q):
        for m in range(pair_chunks):
            arrive(pair.at[q, m], sp_sem.at[q, m], rp_sem.at[q, m], {"dp": partner})

    place_z = z // 2

    def pair_at(d):
        return lax.rem(place_z + d + 2 * n_pairs, n_pairs)

    def make_term(target):
        q, m = target // pair_chunks, lax.rem(target, pair_chunks)
        mine = columns(q, m, z_side)[...].reshape(n_slots, chunk_cols)
        theirs = pair[q, m].reshape(n_slots, chunk_cols)
        total = dot(acts[0], mine) + dot(acts[1], theirs)
        term[target] = total.reshape(SUB, hidden // SUB, chunk_cols)

    def z_send(way, s, i):
        send(
            zout.at[way, s, i],
            zin.at[way, s, i],
            sz_sem.at[way, s, i],
            rz_sem.at[way, s, i],
            {"dp": z_up if way == 0 else z_down},
        )

    def z_arrive(way, s, i):
        arrive(
            zin.at[way, s, i],
            sz_sem.at[way, s, i],
            rz_sem.at[way, s, i],
            {"dp": z_down if way == 0 else z_up},
        )
        return zin[way, s, i].astype(F32)

    def z_step(s):
        targets = (pair_at(half_z - s), pair_at(s - half_z))
        for j in range(SUB if s > 0 else SUB // 2):
            early = j < SUB // 2
            for way in range(2):
                i = j if way == 0 else SUB - 1 - j
                value = term[targets[way], i]
                if s > 1 or (s == 1 and early):
                    value = value + z_arrive(way, s - 1, i)
                zout[way, s, i] = value.astype(BF16)
                z_send(way, s, i)

    def z_finish():
        for i in range(SUB):
            total = term[place_z, i] + z_arrive(0, half_z - 1, i) + z_arrive(1, half_z - 1, i)
            rows_here = hidden // SUB
            gd_out[pl.ds(i * rows_here, rows_here), :] = (total * (1.0 / n_z)).astype(BF16)
        store = pltpu.make_async_copy(gd_out, gd_hbm, out_sem.at[2])
        store.start()
        stores.append(store)

    def gate_up(q):
        block = row_block(0, q)
        return dot_t(block, weight(gw, q)), dot_t(block, weight(uw, q))

    def act_grad(q):
        return dot_t(row_block(1, q), weight(dw, q))

    def down_part(q):
        put_part(0, q, dot(act_b, weight(dw, q)))

    def input_part(q):
        put_part(1, q, dot(gate_back, weight(gw, q)) + dot(up_back, weight(uw, q)))

    dispatch(0)
    dispatch(1)
    dispatch_wait(0)
    gather_start(0, 0)
    gather_start(0, 1)
    loads[0].wait()
    loads[1].wait()
    gate_s[...], up_s[...] = gate_up(x)
    dispatch_wait(1)
    gather_start(1, 0)
    gather_relay(0)
    gather_start(1, 1)
    pair_send(x)
    gather_near(0)
    for q in (left, right):
        gate, up = gate_up(q)
        gate_s[...] += gate
        up_s[...] += up
    gather_relay(1)
    gather_far(0)
    gate, up = gate_up(far)
    gate = gate_s[...] + gate
    up = up_s[...] + up
    squash = 1.0 / (1.0 + jnp.exp(-gate))
    swish = gate * squash
    act = swish * up
    gate_s[...] = up * squash * (1.0 + gate * (1.0 - squash))
    up_s[...] = swish
    act_b = act.astype(BF16)
    acts[0] = act.T.astype(BF16)
    act_send()
    loads[2].wait()
    gather_near(1)
    pair_send(left)
    pair_send(right)
    down_part(far)
    reduce_far(0)
    down_part(right)
    down_part(left)
    reduce_near(0)
    grad = act_grad(x) + act_grad(left) + act_grad(right)
    gather_far(1)
    pair_send(far)
    grad = grad + act_grad(far)
    gate_back = (grad * gate_s[...]).astype(BF16)
    up_back = (grad * up_s[...]).astype(BF16)
    input_part(far)
    reduce_far(1)
    down_part(x)
    reduce_relay(0)
    act_arrive()
    for q in (x, left, right, far):
        pair_arrive(q)
    make_term(pair_at(half_z))
    z_step(0)
    make_term(pair_at(half_z - 1))
    make_term(pair_at(1 - half_z))
    input_part(right)
    input_part(left)
    reduce_near(1)
    z_step(1)
    for s in range(2, half_z):
        make_term(pair_at(half_z - s))
        make_term(pair_at(s - half_z))
    make_term(place_z)
    reduce_end(0)
    input_part(x)
    reduce_relay(1)
    z_step(2)
    reduce_end(1)
    combine(0)
    for s in range(3, half_z):
        z_step(s)
    combine(1)
    z_finish()
    finish(0)
    finish(1)
    for store in stores:
        store.wait()
    for copy in started:
        copy.wait_send()


def shards(
    tokens, routes, positions, combine_weights, cotangent, gate_weight, up_weight, down_weight
):
    n_z, n_e, n_x = lax.axis_size("dp"), lax.axis_size("expert"), lax.axis_size("tensor")
    tokens_here, width = tokens.shape
    group_size = routes.shape[0]
    cap = group_size // 2
    hidden = gate_weight.shape[2]
    q_cols = width // n_x
    n_slots = n_e * cap
    half_e, n_pairs = n_e // 2, n_z // 2
    half_z = n_pairs // 2
    pair_chunks = n_pairs // n_x
    z_rows = width // n_z
    hbm = pl.BlockSpec(memory_space=pl.ANY)
    dma = pltpu.SemaphoreType.DMA
    weights = [jnp.swapaxes(w[0], 0, 1) for w in (gate_weight, up_weight, down_weight)]
    plans = [v.T for v in (routes, positions, combine_weights)]
    quarter = (half_e, cap, q_cols)
    return pl.pallas_call(
        functools.partial(kernel, n_z, n_e),
        out_shape=(
            jax.ShapeDtypeStruct((tokens_here, width), BF16),
            jax.ShapeDtypeStruct((tokens_here, width), BF16),
            jax.ShapeDtypeStruct((hidden, z_rows), BF16),
        ),
        in_specs=[hbm] * 8,
        out_specs=(hbm, hbm, hbm),
        scratch_shapes=[pltpu.VMEM(v.shape, v.dtype) for v in (tokens, cotangent, *plans)]
        + [pltpu.VMEM((hidden, width), BF16)] * 3
        + [
            pltpu.VMEM((2, n_x, tokens_here, q_cols), BF16),
            pltpu.VMEM((group_size, q_cols), F32),
            pltpu.VMEM((2, 2) + quarter, BF16),
            pltpu.VMEM((2, n_x, 2) + quarter, BF16),
            pltpu.VMEM((n_slots, hidden), F32),
            pltpu.VMEM((n_slots, hidden), F32),
            pltpu.VMEM((2, n_x, 2) + quarter, BF16),
            pltpu.VMEM((2, 2) + quarter, BF16),
            pltpu.VMEM((2, 2) + quarter, BF16),
            pltpu.VMEM((2, 2, 2) + quarter, BF16),
            pltpu.VMEM((2, 2) + quarter, BF16),
            pltpu.VMEM((2, 2) + quarter, BF16),
            pltpu.VMEM((2, n_x, tokens_here, q_cols), BF16),
            pltpu.VMEM((2, hidden, n_slots), BF16),
            pltpu.VMEM((n_x, pair_chunks, 2, half_e, cap, z_rows), BF16),
            pltpu.VMEM((n_pairs, SUB, hidden // SUB, z_rows), F32),
            pltpu.VMEM((2, half_z, SUB, hidden // SUB, z_rows), BF16),
            pltpu.VMEM((2, half_z, SUB, hidden // SUB, z_rows), BF16),
            pltpu.VMEM((hidden, z_rows), BF16),
            dma((5,)),
            dma((3,)),
            dma((3,)),
            dma((2, n_x)),
            dma((2, n_x)),
            dma((2, n_e)),
            dma((2, n_e)),
            dma((2, 3, 2)),
            dma((2, 3, 2)),
            dma((2, 6)),
            dma((2, 6)),
            dma((2, n_e)),
            dma((2, n_e)),
            dma((2, n_x)),
            dma((2, n_x)),
            dma((1,)),
            dma((1,)),
            dma((n_x, pair_chunks)),
            dma((n_x, pair_chunks)),
            dma((2, half_z, SUB)),
            dma((2, half_z, SUB)),
        ],
        compiler_params=pltpu.CompilerParams(
            collective_id=0, has_side_effects=True, vmem_limit_bytes=56 * 1024 * 1024
        ),
    )(tokens, cotangent, *plans, *weights)


def place(*refs):
    half = len(refs) // 2
    for source, target in zip(refs[:half], refs[half:]):
        target[...] = source[...]


def body(*arrays):
    results = shards(*arrays)
    layer_out, grad_tokens, grad_down = pl.pallas_call(
        place,
        out_shape=tuple(jax.ShapeDtypeStruct(r.shape, r.dtype) for r in results),
        in_specs=[pl.BlockSpec(memory_space=pltpu.VMEM)] * 3,
        out_specs=(pl.BlockSpec(memory_space=pltpu.VMEM),) * 3,
    )(*results)
    return layer_out, grad_tokens, jnp.swapaxes(grad_down, 0, 1)[None]


def solution(mesh):
    return jax.shard_map(
        body,
        mesh=mesh,
        in_specs=(
            P(("dp", "expert", "tensor"), None),
            P(("dp", "expert"), None),
            P(("dp", "expert"), None),
            P(("dp", "expert"), None),
            P(("dp", "expert", "tensor"), None),
            P("expert", None, "tensor"),
            P("expert", None, "tensor"),
            P("expert", None, "tensor"),
        ),
        out_specs=(
            P(("dp", "expert", "tensor"), None),
            P(("dp", "expert", "tensor"), None),
            P("expert", "dp", "tensor"),
        ),
        check_vma=False,
    )
```

```python
import functools

import jax
import jax.numpy as jnp
from jax import lax
from jax.experimental import pallas as pl
from jax.experimental.pallas import tpu as pltpu
from jax.sharding import PartitionSpec as P

MESH = pl.DeviceIdType.MESH
F32 = jnp.float32
BF16 = jnp.bfloat16
SUB = 4
UP_SUB = SUB // 2
PIECES = 4


def dot(left, right):
    return lax.dot_general(left, right, (((1,), (0,)), ((), ())), preferred_element_type=F32)


def dot_t(left, right):
    return lax.dot_general(left, right, (((1,), (1,)), ((), ())), preferred_element_type=F32)


def kernel(
    n_z,
    n_e,
    tok_hbm,
    cot_hbm,
    routes_hbm,
    pos_hbm,
    cw_hbm,
    gw_hbm,
    uw_hbm,
    dw_hbm,
    lo_hbm,
    gt_hbm,
    gd_hbm,
    tok_ref,
    cot_ref,
    routes_ref,
    pos_ref,
    cw_ref,
    gw,
    uw,
    dw,
    xin,
    group,
    dsend,
    rows,
    gate_s,
    up_s,
    part,
    rs_far,
    rs_sum,
    rs_near,
    ysend,
    yret,
    csend,
    acts,
    pair,
    term,
    zin,
    zout,
    gd_out,
    in_sem,
    out_sem,
    w_sem,
    sx_sem,
    rx_sem,
    sd_sem,
    rd_sem,
    sg_sem,
    rg_sem,
    sr_sem,
    rr_sem,
    sy_sem,
    ry_sem,
    sc_sem,
    rc_sem,
    sa_sem,
    ra_sem,
    sp_sem,
    rp_sem,
    sz_sem,
    rz_sem,
):
    n_x, _, _, cap, q_cols = rows.shape[1:]
    tokens_here = tok_ref.shape[0]
    group_size = routes_ref.shape[1]
    n_slots = n_e * cap
    per_piece = n_e // PIECES
    n_pairs = n_z // 2
    half_z = n_pairs // 2
    hidden = gate_s.shape[1]
    x = lax.axis_index("tensor")
    e = lax.axis_index("expert")
    z = lax.axis_index("dp")

    def x_at(d):
        return lax.rem(x + d + n_x, n_x)

    def e_at(d):
        return lax.rem(e + d + n_e, n_e)

    def z_at(d):
        return lax.rem(z + d + 2 * n_z, n_z)

    started = []

    def send(src, dst, send_sem, recv_sem, device):
        copy = pltpu.make_async_remote_copy(
            src_ref=src,
            dst_ref=dst,
            send_sem=send_sem,
            recv_sem=recv_sem,
            device_id=device,
            device_id_type=MESH,
        )
        copy.start()
        started.append(copy)

    def arrive(dst, send_sem, recv_sem, device):
        pltpu.make_async_remote_copy(
            src_ref=dst,
            dst_ref=dst,
            send_sem=send_sem,
            recv_sem=recv_sem,
            device_id=device,
            device_id_type=MESH,
        ).wait_recv()

    fetches = []
    for i, (src, dst) in enumerate(
        (
            (routes_hbm, routes_ref),
            (pos_hbm, pos_ref),
            (cw_hbm, cw_ref),
            (tok_hbm, tok_ref),
            (cot_hbm, cot_ref),
        )
    ):
        fetch = pltpu.make_async_copy(src, dst, in_sem.at[i])
        fetch.start()
        fetches.append(fetch)
    barrier = pltpu.get_barrier_semaphore()
    for d in range(1, n_x):
        pl.semaphore_signal(barrier, inc=1, device_id={"tensor": x_at(d)}, device_id_type=MESH)
    for d in range(1, n_e):
        pl.semaphore_signal(barrier, inc=1, device_id={"expert": e_at(d)}, device_id_type=MESH)
    z_side = lax.rem(z, 2)
    partner = z + 1 - 2 * z_side
    z_up, z_down = z_at(2), z_at(-2)
    for to in (partner, z_up, z_down):
        pl.semaphore_signal(barrier, inc=1, device_id={"dp": to}, device_id_type=MESH)
    loads = []
    for i, (src, dst) in enumerate(((gw_hbm, gw), (uw_hbm, uw), (dw_hbm, dw))):
        load = pltpu.make_async_copy(src, dst, w_sem.at[i])
        load.start()
        loads.append(load)

    for fetch in fetches:
        fetch.wait()
    pl.semaphore_wait(barrier, n_x - 1 + n_e - 1 + 3)

    sources = (tok_ref, cot_ref)

    def quarter_of(a, q):
        return sources[a].at[:, pl.ds(pl.multiple_of(q * q_cols, q_cols), q_cols)]

    for a in range(2):
        for d in range(1, n_x):
            q = x_at(d)
            send(
                quarter_of(a, q),
                xin.at[a, x],
                sx_sem.at[a, d],
                rx_sem.at[a, d],
                {"tensor": q},
            )
    for a in range(2):
        xin[a, x] = quarter_of(a, x)[...]

    slot_ids = routes_ref[...] * cap + pos_ref[...]
    gains = cw_ref[...]
    numbers = lax.broadcasted_iota(jnp.int32, (n_slots, group_size), 0)
    placed = jnp.zeros((n_slots, group_size), F32)
    weighted = jnp.zeros((n_slots, group_size), F32)
    for k in range(slot_ids.shape[0]):
        match = numbers == slot_ids[k : k + 1, :]
        placed = placed + jnp.where(match, 1.0, 0.0)
        weighted = weighted + jnp.where(match, gains[k : k + 1, :], 0.0)

    def pieces(table):
        high = table.astype(BF16)
        return high, (table - high.astype(F32)).astype(BF16)

    placed_in = placed.astype(BF16)
    weighted_in = pieces(weighted)
    placed_back = placed.T.astype(BF16)
    weighted_back = pieces(weighted.T)

    near_first = [d for k in range(1, n_e // 2 + 1) for d in sorted({k, n_e - k})]

    def rows_at(a, q, r):
        return rows.at[a, q, r // per_piece, r % per_piece]

    def dispatch(a):
        for d in range(1, n_x):
            src = x_at(-d)
            arrive(xin.at[a, src], sx_sem.at[a, d], rx_sem.at[a, d], {"tensor": src})
        for j in range(n_x):
            group[pl.ds(j * tokens_here, tokens_here), :] = xin[a, j].astype(F32)
        here = group[...].astype(BF16)
        if a == 0:
            slots = dot(placed_in, here)
        else:
            slots = dot(weighted_in[0], here) + dot(weighted_in[1], here)
        dsend[a] = slots.reshape(n_e, cap, q_cols).astype(BF16)
        for d in near_first:
            to = e_at(d)
            send(
                dsend.at[a, to],
                rows_at(a, x, n_e - d),
                sd_sem.at[a, d],
                rd_sem.at[a, d],
                {"expert": to},
            )
        rows[a, x, 0, 0] = dsend[a, e]

    def dispatch_wait(a, p):
        for r in range(max(1, p * per_piece), (p + 1) * per_piece):
            d = n_e - r
            arrive(rows_at(a, x, r), sd_sem.at[a, d], rd_sem.at[a, d], {"expert": e_at(r)})

    right, left = x_at(1), x_at(-1)
    far = x_at(2)

    def gathered(a, q, p):
        return rows.at[a, q, p] if a < 2 else pair.at[q, :, p]

    def gather_send(a, q, p, to, way, hop):
        ref = gathered(a, q, p)
        send(ref, ref, sg_sem.at[a, way, hop, p], rg_sem.at[a, way, hop, p], {"tensor": to})

    def gather_wait(a, q, p, way, hop):
        origin = left if way == 0 else right
        arrive(gathered(a, q, p), sg_sem.at[a, way, hop, p], rg_sem.at[a, way, hop, p], {"tensor": origin})

    relay_right, relay_left = (0, 1), (3, 2)

    def gather_start(a, k):
        gather_send(a, x, relay_right[k], right, 0, 0)
        gather_send(a, x, relay_left[k], left, 1, 0)

    def gather_rest(a, k):
        gather_send(a, x, relay_left[k], right, 0, 0)
        gather_send(a, x, relay_right[k], left, 1, 0)

    def gather_relay(a, k):
        p = relay_right[k]
        gather_wait(a, left, p, 0, 0)
        gather_send(a, left, p, right, 0, 1)
        p = relay_left[k]
        gather_wait(a, right, p, 1, 0)
        gather_send(a, right, p, left, 1, 1)

    def gather_near(a):
        for k in range(2):
            gather_wait(a, left, relay_left[k], 0, 0)
            gather_wait(a, right, relay_right[k], 1, 0)

    def gather_far(a):
        for k in range(2):
            gather_wait(a, far, relay_right[k], 0, 1)
            gather_wait(a, far, relay_left[k], 1, 1)

    def weight(ref, q):
        return ref[:, pl.ds(pl.multiple_of(q * q_cols, q_cols), q_cols)]

    def row_block(a, q):
        return rows[a, q].reshape(n_slots, q_cols)

    def put_part(b, q, value):
        part[b, q] = value.reshape(n_e, cap, q_cols).astype(BF16).reshape(PIECES, per_piece, cap, q_cols)

    def reduce_send(b, src, dst, way, hop, p):
        to = right if way == 0 else left
        send(src, dst, sr_sem.at[b, way, hop, p], rr_sem.at[b, way, hop, p], {"tensor": to})

    def reduce_wait(b, dst, way, hop, p):
        origin = left if way == 0 else right
        arrive(dst, sr_sem.at[b, way, hop, p], rr_sem.at[b, way, hop, p], {"tensor": origin})

    def reduce_far(b):
        for k in range(2):
            p = relay_right[k]
            reduce_send(b, part.at[b, far, p], rs_far.at[b, p], 0, 0, p)
            p = relay_left[k]
            reduce_send(b, part.at[b, far, p], rs_far.at[b, p], 1, 0, p)

    def reduce_near(b):
        for k in range(2):
            p = relay_left[k]
            reduce_send(b, part.at[b, right, p], rs_near.at[b, 0, p], 0, 1, p)
            p = relay_right[k]
            reduce_send(b, part.at[b, left, p], rs_near.at[b, 1, p], 1, 1, p)

    def reduce_relay(b):
        for k in range(2):
            for way, p in ((0, relay_right[k]), (1, relay_left[k])):
                onward = right if way == 0 else left
                reduce_wait(b, rs_far.at[b, p], way, 0, p)
                rs_sum[b, p] = (rs_far[b, p].astype(F32) + part[b, onward, p].astype(F32)).astype(BF16)
                reduce_send(b, rs_sum.at[b, p], rs_near.at[b, way, p], way, 1, p)

    def reduce_end(b):
        for p in (0, 3, 1, 2):
            for way in range(2):
                reduce_wait(b, rs_near.at[b, way, p], way, 1, p)
            total = part[b, x, p].astype(F32) + rs_near[b, 0, p].astype(F32) + rs_near[b, 1, p].astype(F32)
            ysend[b, p] = total.astype(BF16)
            for i in range(per_piece):
                r = p * per_piece + i
                if r == 0:
                    yret[b, e] = ysend[b, 0, 0]
                    continue
                send(
                    ysend.at[b, p, i],
                    yret.at[b, e],
                    sy_sem.at[b, r],
                    ry_sem.at[b, r],
                    {"expert": e_at(r)},
                )

    stores = []
    results = (lo_hbm, gt_hbm)

    def result_of(b, q):
        return results[b].at[:, pl.ds(pl.multiple_of(q * q_cols, q_cols), q_cols)]

    def combine(b):
        for d in range(1, n_e):
            src = e_at(-d)
            arrive(yret.at[b, src], sy_sem.at[b, d], ry_sem.at[b, d], {"expert": src})
        slots = yret[b].reshape(n_slots, q_cols)
        if b == 0:
            mixed = dot(weighted_back[0], slots) + dot(weighted_back[1], slots)
        else:
            mixed = dot(placed_back, slots)
        group[...] = mixed
        for j in range(n_x):
            csend[b, j] = group[pl.ds(j * tokens_here, tokens_here), :].astype(BF16)
        for d in range(1, n_x):
            to = x_at(d)
            send(csend.at[b, to], result_of(b, x), sc_sem.at[b, d], rc_sem.at[b, d], {"tensor": to})
        own = pltpu.make_async_copy(csend.at[b, x], result_of(b, x), out_sem.at[b])
        own.start()
        stores.append(own)

    def finish(b):
        for d in range(1, n_x):
            src = x_at(-d)
            arrive(result_of(b, src), sc_sem.at[b, d], rc_sem.at[b, d], {"tensor": src})

    chunk_cols = term.shape[3]
    pair_chunks = q_cols // chunk_cols // 2

    def act_send():
        send(acts.at[0], acts.at[1], sa_sem.at[0], ra_sem.at[0], {"dp": partner})

    def act_arrive():
        arrive(acts.at[1], sa_sem.at[0], ra_sem.at[0], {"dp": partner})

    def columns(q, m, side):
        start = pl.multiple_of((2 * m + side) * chunk_cols, chunk_cols)
        return rows.at[1, q, :, :, :, pl.ds(start, chunk_cols)]

    def pair_send():
        for m in range(pair_chunks):
            send(columns(x, m, 1 - z_side), pair.at[x, m], sp_sem.at[m], rp_sem.at[m], {"dp": partner})

    def pair_arrive():
        for m in range(pair_chunks):
            arrive(pair.at[x, m], sp_sem.at[m], rp_sem.at[m], {"dp": partner})

    place_z = z // 2

    def pair_at(d):
        return lax.rem(place_z + d + 2 * n_pairs, n_pairs)

    def make_term(target):
        q, m = target // pair_chunks, lax.rem(target, pair_chunks)
        mine = columns(q, m, z_side)[...].reshape(n_slots, chunk_cols)
        theirs = pair[q, m].reshape(n_slots, chunk_cols)
        total = dot(acts[0], mine) + dot(acts[1], theirs)
        term[target] = total.reshape(SUB, hidden // SUB, chunk_cols)

    def z_send(way, s, i):
        send(
            zout.at[way, s, i],
            zin.at[way, s, i],
            sz_sem.at[way, s, i],
            rz_sem.at[way, s, i],
            {"dp": z_up if way == 0 else z_down},
        )

    def z_arrive(way, s, i):
        arrive(
            zin.at[way, s, i],
            sz_sem.at[way, s, i],
            rz_sem.at[way, s, i],
            {"dp": z_down if way == 0 else z_up},
        )
        return zin[way, s, i].astype(F32)

    def z_step(s, first):
        targets = (pair_at(half_z - s), pair_at(s - half_z))
        for j in range(SUB):
            for way in range(2):
                i = j if way == 0 else SUB - 1 - j
                early = j < (UP_SUB if way == 0 else SUB - UP_SUB)
                if early != first:
                    continue
                value = term[targets[way], i]
                if s > 1 or (s == 1 and early):
                    value = value + z_arrive(way, s - 1, i)
                zout[way, s, i] = value.astype(BF16)
                z_send(way, s, i)

    def z_finish():
        for i in range(SUB):
            total = term[place_z, i] + z_arrive(0, half_z - 1, i) + z_arrive(1, half_z - 1, i)
            rows_here = hidden // SUB
            gd_out[pl.ds(i * rows_here, rows_here), :] = (total * (1.0 / n_z)).astype(BF16)
        store = pltpu.make_async_copy(gd_out, gd_hbm, out_sem.at[2])
        store.start()
        stores.append(store)

    def gate_up(q):
        block = row_block(0, q)
        return dot_t(block, weight(gw, q)), dot_t(block, weight(uw, q))

    def act_grad(q):
        return dot_t(row_block(1, q), weight(dw, q))

    def down_part(q):
        put_part(0, q, dot(act_b, weight(dw, q)))

    def input_part(q):
        put_part(1, q, dot(gate_back, weight(gw, q)) + dot(up_back, weight(uw, q)))

    dispatch(0)
    dispatch(1)
    for k in range(2):
        dispatch_wait(0, relay_right[k])
        dispatch_wait(0, relay_left[k])
        gather_start(0, k)
    gather_rest(0, 0)
    gather_rest(0, 1)
    loads[0].wait()
    loads[1].wait()
    gate_s[...], up_s[...] = gate_up(x)
    for k in range(2):
        dispatch_wait(1, relay_right[k])
        dispatch_wait(1, relay_left[k])
        gather_start(1, k)
    pair_send()
    gather_relay(0, 0)
    gather_relay(0, 1)
    gather_rest(1, 0)
    gather_rest(1, 1)
    gather_near(0)
    for q in (left, right):
        gate, up = gate_up(q)
        gate_s[...] += gate
        up_s[...] += up
    gather_relay(1, 0)
    gather_relay(1, 1)
    pair_arrive()
    gather_start(2, 0)
    gather_start(2, 1)
    gather_rest(2, 0)
    gather_rest(2, 1)
    gather_far(0)
    gate, up = gate_up(far)
    gate = gate_s[...] + gate
    up = up_s[...] + up
    squash = 1.0 / (1.0 + jnp.exp(-gate))
    swish = gate * squash
    act = swish * up
    gate_s[...] = up * squash * (1.0 + gate * (1.0 - squash))
    up_s[...] = swish
    act_b = act.astype(BF16)
    acts[0] = act.T.astype(BF16)
    act_send()
    loads[2].wait()
    gather_near(1)
    down_part(far)
    reduce_far(0)
    down_part(right)
    down_part(left)
    gather_relay(2, 0)
    gather_relay(2, 1)
    reduce_near(0)
    grad = act_grad(x) + act_grad(left) + act_grad(right)
    gather_far(1)
    grad = grad + act_grad(far)
    gate_back = (grad * gate_s[...]).astype(BF16)
    up_back = (grad * up_s[...]).astype(BF16)
    input_part(far)
    reduce_far(1)
    act_arrive()
    gather_near(2)
    gather_far(2)
    make_term(pair_at(half_z))
    z_step(0, True)
    make_term(pair_at(half_z - 1))
    make_term(pair_at(1 - half_z))
    z_step(1, False)
    reduce_relay(0)
    input_part(right)
    input_part(left)
    reduce_near(1)
    for s in range(2, half_z):
        make_term(pair_at(half_z - s))
        make_term(pair_at(s - half_z))
    make_term(place_z)
    down_part(x)
    input_part(x)
    reduce_relay(1)
    reduce_end(0)
    z_step(1, True)
    z_step(2, False)
    reduce_end(1)
    z_step(2, True)
    combine(0)
    z_step(3, False)
    combine(1)
    z_step(3, True)
    finish(0)
    finish(1)
    z_finish()
    for store in stores:
        store.wait()
    for copy in started:
        copy.wait_send()


def shards(
    tokens, routes, positions, combine_weights, cotangent, gate_weight, up_weight, down_weight
):
    n_z, n_e, n_x = lax.axis_size("dp"), lax.axis_size("expert"), lax.axis_size("tensor")
    tokens_here, width = tokens.shape
    group_size = routes.shape[0]
    cap = group_size // 2
    hidden = gate_weight.shape[2]
    q_cols = width // n_x
    n_slots = n_e * cap
    per_piece, n_pairs = n_e // PIECES, n_z // 2
    half_z = n_pairs // 2
    pair_chunks = n_pairs // n_x
    z_rows = width // n_z
    hbm = pl.BlockSpec(memory_space=pl.ANY)
    dma = pltpu.SemaphoreType.DMA
    weights = [jnp.swapaxes(w[0], 0, 1) for w in (gate_weight, up_weight, down_weight)]
    plans = [v.T for v in (routes, positions, combine_weights)]
    quarter = (PIECES, per_piece, cap, q_cols)
    slots = (n_e, cap, q_cols)
    return pl.pallas_call(
        functools.partial(kernel, n_z, n_e),
        out_shape=(
            jax.ShapeDtypeStruct((tokens_here, width), BF16),
            jax.ShapeDtypeStruct((tokens_here, width), BF16),
            jax.ShapeDtypeStruct((hidden, z_rows), BF16),
        ),
        in_specs=[hbm] * 8,
        out_specs=(hbm, hbm, hbm),
        scratch_shapes=[pltpu.VMEM(v.shape, v.dtype) for v in (tokens, cotangent, *plans)]
        + [pltpu.VMEM((hidden, width), BF16)] * 3
        + [
            pltpu.VMEM((2, n_x, tokens_here, q_cols), BF16),
            pltpu.VMEM((group_size, q_cols), F32),
            pltpu.VMEM((2,) + slots, BF16),
            pltpu.VMEM((2, n_x) + quarter, BF16),
            pltpu.VMEM((n_slots, hidden), F32),
            pltpu.VMEM((n_slots, hidden), F32),
            pltpu.VMEM((2, n_x) + quarter, BF16),
            pltpu.VMEM((2,) + quarter, BF16),
            pltpu.VMEM((2,) + quarter, BF16),
            pltpu.VMEM((2, 2) + quarter, BF16),
            pltpu.VMEM((2,) + quarter, BF16),
            pltpu.VMEM((2,) + slots, BF16),
            pltpu.VMEM((2, n_x, tokens_here, q_cols), BF16),
            pltpu.VMEM((2, hidden, n_slots), BF16),
            pltpu.VMEM((n_x, pair_chunks, PIECES, per_piece, cap, z_rows), BF16),
            pltpu.VMEM((n_pairs, SUB, hidden // SUB, z_rows), F32),
            pltpu.VMEM((2, half_z, SUB, hidden // SUB, z_rows), BF16),
            pltpu.VMEM((2, half_z, SUB, hidden // SUB, z_rows), BF16),
            pltpu.VMEM((hidden, z_rows), BF16),
            dma((5,)),
            dma((3,)),
            dma((3,)),
            dma((2, n_x)),
            dma((2, n_x)),
            dma((2, n_e)),
            dma((2, n_e)),
            dma((3, 2, 2, PIECES)),
            dma((3, 2, 2, PIECES)),
            dma((2, 2, 2, PIECES)),
            dma((2, 2, 2, PIECES)),
            dma((2, n_e)),
            dma((2, n_e)),
            dma((2, n_x)),
            dma((2, n_x)),
            dma((1,)),
            dma((1,)),
            dma((pair_chunks,)),
            dma((pair_chunks,)),
            dma((2, half_z, SUB)),
            dma((2, half_z, SUB)),
        ],
        compiler_params=pltpu.CompilerParams(
            collective_id=0, has_side_effects=True, vmem_limit_bytes=56 * 1024 * 1024
        ),
    )(tokens, cotangent, *plans, *weights)


def place(*refs):
    half = len(refs) // 2
    for source, target in zip(refs[:half], refs[half:]):
        target[...] = source[...]


def body(*arrays):
    results = shards(*arrays)
    layer_out, grad_tokens, grad_down = pl.pallas_call(
        place,
        out_shape=tuple(jax.ShapeDtypeStruct(r.shape, r.dtype) for r in results),
        in_specs=[pl.BlockSpec(memory_space=pltpu.VMEM)] * 3,
        out_specs=(pl.BlockSpec(memory_space=pltpu.VMEM),) * 3,
    )(*results)
    return layer_out, grad_tokens, jnp.swapaxes(grad_down, 0, 1)[None]


def solution(mesh):
    return jax.shard_map(
        body,
        mesh=mesh,
        in_specs=(
            P(("dp", "expert", "tensor"), None),
            P(("dp", "expert"), None),
            P(("dp", "expert"), None),
            P(("dp", "expert"), None),
            P(("dp", "expert", "tensor"), None),
            P("expert", None, "tensor"),
            P("expert", None, "tensor"),
            P("expert", None, "tensor"),
        ),
        out_specs=(
            P(("dp", "expert", "tensor"), None),
            P(("dp", "expert", "tensor"), None),
            P("expert", "dp", "tensor"),
        ),
        check_vma=False,
    )
```

```python
import functools

import jax
import jax.numpy as jnp
from jax import lax
from jax.experimental import pallas as pl
from jax.experimental.pallas import tpu as pltpu
from jax.sharding import PartitionSpec as P

MESH = pl.DeviceIdType.MESH
F32 = jnp.float32
BF16 = jnp.bfloat16
SUB = 2
UP_SUB = SUB // 2
PIECES = 4


def dot(left, right):
    return lax.dot_general(left, right, (((1,), (0,)), ((), ())), preferred_element_type=F32)


def dot_t(left, right):
    return lax.dot_general(left, right, (((1,), (1,)), ((), ())), preferred_element_type=F32)


def kernel(
    n_z,
    n_e,
    tok_hbm,
    cot_hbm,
    routes_hbm,
    pos_hbm,
    cw_hbm,
    gw_hbm,
    uw_hbm,
    dw_hbm,
    lo_hbm,
    gt_hbm,
    gd_hbm,
    tok_ref,
    cot_ref,
    routes_ref,
    pos_ref,
    cw_ref,
    gw,
    uw,
    dw,
    xin,
    group,
    dsend,
    rows,
    gate_s,
    up_s,
    part,
    rs_far,
    rs_sum,
    rs_near,
    ysend,
    yret,
    csend,
    acts,
    pair,
    term,
    zin,
    zout,
    gd_out,
    in_sem,
    out_sem,
    w_sem,
    sx_sem,
    rx_sem,
    sd_sem,
    rd_sem,
    sg_sem,
    rg_sem,
    sr_sem,
    rr_sem,
    sy_sem,
    ry_sem,
    sc_sem,
    rc_sem,
    sa_sem,
    ra_sem,
    sp_sem,
    rp_sem,
    sz_sem,
    rz_sem,
):
    n_x, _, _, cap, q_cols = rows.shape[1:]
    tokens_here = tok_ref.shape[0]
    group_size = routes_ref.shape[1]
    n_slots = n_e * cap
    per_piece = n_e // PIECES
    n_pairs = n_z // 2
    half_z = n_pairs // 2
    hidden = gate_s.shape[1]
    x = lax.axis_index("tensor")
    e = lax.axis_index("expert")
    z = lax.axis_index("dp")

    def x_at(d):
        return lax.rem(x + d + n_x, n_x)

    def e_at(d):
        return lax.rem(e + d + n_e, n_e)

    def z_at(d):
        return lax.rem(z + d + 2 * n_z, n_z)

    started = []

    def send(src, dst, send_sem, recv_sem, device):
        copy = pltpu.make_async_remote_copy(
            src_ref=src,
            dst_ref=dst,
            send_sem=send_sem,
            recv_sem=recv_sem,
            device_id=device,
            device_id_type=MESH,
        )
        copy.start()
        started.append(copy)

    def arrive(dst, send_sem, recv_sem, device):
        pltpu.make_async_remote_copy(
            src_ref=dst,
            dst_ref=dst,
            send_sem=send_sem,
            recv_sem=recv_sem,
            device_id=device,
            device_id_type=MESH,
        ).wait_recv()

    fetches = []
    for i, (src, dst) in enumerate(
        (
            (routes_hbm, routes_ref),
            (pos_hbm, pos_ref),
            (cw_hbm, cw_ref),
            (tok_hbm, tok_ref),
            (cot_hbm, cot_ref),
        )
    ):
        fetch = pltpu.make_async_copy(src, dst, in_sem.at[i])
        fetch.start()
        fetches.append(fetch)
    barrier = pltpu.get_barrier_semaphore()
    for d in range(1, n_x):
        pl.semaphore_signal(barrier, inc=1, device_id={"tensor": x_at(d)}, device_id_type=MESH)
    for d in range(1, n_e):
        pl.semaphore_signal(barrier, inc=1, device_id={"expert": e_at(d)}, device_id_type=MESH)
    z_side = lax.rem(z, 2)
    partner = z + 1 - 2 * z_side
    z_up, z_down = z_at(2), z_at(-2)
    for to in (partner, z_up, z_down):
        pl.semaphore_signal(barrier, inc=1, device_id={"dp": to}, device_id_type=MESH)
    loads = []
    for i, (src, dst) in enumerate(((gw_hbm, gw), (uw_hbm, uw), (dw_hbm, dw))):
        load = pltpu.make_async_copy(src, dst, w_sem.at[i])
        load.start()
        loads.append(load)

    for fetch in fetches:
        fetch.wait()
    pl.semaphore_wait(barrier, n_x - 1 + n_e - 1 + 3)

    sources = (tok_ref, cot_ref)

    def quarter_of(a, q):
        return sources[a].at[:, pl.ds(pl.multiple_of(q * q_cols, q_cols), q_cols)]

    for a in range(2):
        for d in range(1, n_x):
            q = x_at(d)
            send(
                quarter_of(a, q),
                xin.at[a, x],
                sx_sem.at[a, d],
                rx_sem.at[a, d],
                {"tensor": q},
            )
    for a in range(2):
        xin[a, x] = quarter_of(a, x)[...]

    slot_ids = routes_ref[...] * cap + pos_ref[...]
    gains = cw_ref[...]
    numbers = lax.broadcasted_iota(jnp.int32, (n_slots, group_size), 0)
    placed = jnp.zeros((n_slots, group_size), F32)
    weighted = jnp.zeros((n_slots, group_size), F32)
    for k in range(slot_ids.shape[0]):
        match = numbers == slot_ids[k : k + 1, :]
        placed = placed + jnp.where(match, 1.0, 0.0)
        weighted = weighted + jnp.where(match, gains[k : k + 1, :], 0.0)

    def pieces(table):
        high = table.astype(BF16)
        return high, (table - high.astype(F32)).astype(BF16)

    placed_in = placed.astype(BF16)
    weighted_in = pieces(weighted)
    placed_back = placed.T.astype(BF16)
    weighted_back = pieces(weighted.T)

    near_first = [d for k in range(1, n_e // 2 + 1) for d in sorted({k, n_e - k})]

    def rows_at(a, q, r):
        return rows.at[a, q, r // per_piece, r % per_piece]

    def dispatch(a):
        for d in range(1, n_x):
            src = x_at(-d)
            arrive(xin.at[a, src], sx_sem.at[a, d], rx_sem.at[a, d], {"tensor": src})
        for j in range(n_x):
            group[pl.ds(j * tokens_here, tokens_here), :] = xin[a, j].astype(F32)
        here = group[...].astype(BF16)
        if a == 0:
            slots = dot(placed_in, here)
        else:
            slots = dot(weighted_in[0], here) + dot(weighted_in[1], here)
        dsend[a] = slots.reshape(n_e, cap, q_cols).astype(BF16)
        for d in near_first:
            to = e_at(d)
            send(
                dsend.at[a, to],
                rows_at(a, x, n_e - d),
                sd_sem.at[a, d],
                rd_sem.at[a, d],
                {"expert": to},
            )
        rows[a, x, 0, 0] = dsend[a, e]

    def dispatch_wait(a, p):
        for r in range(max(1, p * per_piece), (p + 1) * per_piece):
            d = n_e - r
            arrive(rows_at(a, x, r), sd_sem.at[a, d], rd_sem.at[a, d], {"expert": e_at(r)})

    right, left = x_at(1), x_at(-1)
    far = x_at(2)

    def gathered(a, q, p):
        return rows.at[a, q, p] if a < 2 else pair.at[q, :, p]

    def gather_send(a, q, p, to, way, hop):
        ref = gathered(a, q, p)
        send(ref, ref, sg_sem.at[a, way, hop, p], rg_sem.at[a, way, hop, p], {"tensor": to})

    def gather_wait(a, q, p, way, hop):
        origin = left if way == 0 else right
        arrive(gathered(a, q, p), sg_sem.at[a, way, hop, p], rg_sem.at[a, way, hop, p], {"tensor": origin})

    relay_right, relay_left = (0, 1), (3, 2)

    def gather_start(a, k):
        gather_send(a, x, relay_right[k], right, 0, 0)
        gather_send(a, x, relay_left[k], left, 1, 0)

    def gather_rest(a, k):
        gather_send(a, x, relay_left[k], right, 0, 0)
        gather_send(a, x, relay_right[k], left, 1, 0)

    def gather_relay(a, k):
        p = relay_right[k]
        gather_wait(a, left, p, 0, 0)
        gather_send(a, left, p, right, 0, 1)
        p = relay_left[k]
        gather_wait(a, right, p, 1, 0)
        gather_send(a, right, p, left, 1, 1)

    def gather_near(a):
        for k in range(2):
            gather_wait(a, left, relay_left[k], 0, 0)
            gather_wait(a, right, relay_right[k], 1, 0)

    def gather_far(a):
        for k in range(2):
            gather_wait(a, far, relay_right[k], 0, 1)
            gather_wait(a, far, relay_left[k], 1, 1)

    def weight(ref, q):
        return ref[:, pl.ds(pl.multiple_of(q * q_cols, q_cols), q_cols)]

    def row_block(a, q):
        return rows[a, q].reshape(n_slots, q_cols)

    def put_part(b, q, value):
        part[b, q] = value.reshape(n_e, cap, q_cols).astype(BF16).reshape(PIECES, per_piece, cap, q_cols)

    def reduce_send(b, src, dst, way, hop, p):
        to = right if way == 0 else left
        send(src, dst, sr_sem.at[b, way, hop, p], rr_sem.at[b, way, hop, p], {"tensor": to})

    def reduce_wait(b, dst, way, hop, p):
        origin = left if way == 0 else right
        arrive(dst, sr_sem.at[b, way, hop, p], rr_sem.at[b, way, hop, p], {"tensor": origin})

    def reduce_far(b):
        for k in range(2):
            p = relay_right[k]
            reduce_send(b, part.at[b, far, p], rs_far.at[b, p], 0, 0, p)
            p = relay_left[k]
            reduce_send(b, part.at[b, far, p], rs_far.at[b, p], 1, 0, p)

    def reduce_near(b):
        for k in range(2):
            p = relay_left[k]
            reduce_send(b, part.at[b, right, p], rs_near.at[b, 0, p], 0, 1, p)
            p = relay_right[k]
            reduce_send(b, part.at[b, left, p], rs_near.at[b, 1, p], 1, 1, p)

    def reduce_relay(b):
        for k in range(2):
            for way, p in ((0, relay_right[k]), (1, relay_left[k])):
                onward = right if way == 0 else left
                reduce_wait(b, rs_far.at[b, p], way, 0, p)
                rs_sum[b, p] = (rs_far[b, p].astype(F32) + part[b, onward, p].astype(F32)).astype(BF16)
                reduce_send(b, rs_sum.at[b, p], rs_near.at[b, way, p], way, 1, p)

    def reduce_end(b):
        for p in (0, 3, 1, 2):
            for way in range(2):
                reduce_wait(b, rs_near.at[b, way, p], way, 1, p)
            total = part[b, x, p].astype(F32) + rs_near[b, 0, p].astype(F32) + rs_near[b, 1, p].astype(F32)
            ysend[b, p] = total.astype(BF16)
            for i in range(per_piece):
                r = p * per_piece + i
                if r == 0:
                    yret[b, e] = ysend[b, 0, 0]
                    continue
                send(
                    ysend.at[b, p, i],
                    yret.at[b, e],
                    sy_sem.at[b, r],
                    ry_sem.at[b, r],
                    {"expert": e_at(r)},
                )

    stores = []
    results = (lo_hbm, gt_hbm)

    def result_of(b, q):
        return results[b].at[:, pl.ds(pl.multiple_of(q * q_cols, q_cols), q_cols)]

    def combine(b):
        for d in range(1, n_e):
            src = e_at(-d)
            arrive(yret.at[b, src], sy_sem.at[b, d], ry_sem.at[b, d], {"expert": src})
        slots = yret[b].reshape(n_slots, q_cols)
        if b == 0:
            mixed = dot(weighted_back[0], slots) + dot(weighted_back[1], slots)
        else:
            mixed = dot(placed_back, slots)
        group[...] = mixed
        for j in range(n_x):
            csend[b, j] = group[pl.ds(j * tokens_here, tokens_here), :].astype(BF16)
        for d in range(1, n_x):
            to = x_at(d)
            send(csend.at[b, to], result_of(b, x), sc_sem.at[b, d], rc_sem.at[b, d], {"tensor": to})
        own = pltpu.make_async_copy(csend.at[b, x], result_of(b, x), out_sem.at[b])
        own.start()
        stores.append(own)

    def finish(b):
        for d in range(1, n_x):
            src = x_at(-d)
            arrive(result_of(b, src), sc_sem.at[b, d], rc_sem.at[b, d], {"tensor": src})

    chunk_cols = term.shape[3]
    pair_chunks = q_cols // chunk_cols // 2

    def act_send():
        send(acts.at[0], acts.at[1], sa_sem.at[0], ra_sem.at[0], {"dp": partner})

    def act_arrive():
        arrive(acts.at[1], sa_sem.at[0], ra_sem.at[0], {"dp": partner})

    def columns(q, m, side):
        start = pl.multiple_of((2 * m + side) * chunk_cols, chunk_cols)
        return rows.at[1, q, :, :, :, pl.ds(start, chunk_cols)]

    def pair_send():
        for m in range(pair_chunks):
            send(columns(x, m, 1 - z_side), pair.at[x, m], sp_sem.at[m], rp_sem.at[m], {"dp": partner})

    def pair_arrive():
        for m in range(pair_chunks):
            arrive(pair.at[x, m], sp_sem.at[m], rp_sem.at[m], {"dp": partner})

    place_z = z // 2

    def pair_at(d):
        return lax.rem(place_z + d + 2 * n_pairs, n_pairs)

    def make_term(target):
        q, m = target // pair_chunks, lax.rem(target, pair_chunks)
        mine = columns(q, m, z_side)[...].reshape(n_slots, chunk_cols)
        theirs = pair[q, m].reshape(n_slots, chunk_cols)
        total = dot(acts[0], mine) + dot(acts[1], theirs)
        term[target] = total.reshape(SUB, hidden // SUB, chunk_cols)

    def z_send(way, s, i):
        send(
            zout.at[way, s, i],
            zin.at[way, s, i],
            sz_sem.at[way, s, i],
            rz_sem.at[way, s, i],
            {"dp": z_up if way == 0 else z_down},
        )

    def z_arrive(way, s, i):
        arrive(
            zin.at[way, s, i],
            sz_sem.at[way, s, i],
            rz_sem.at[way, s, i],
            {"dp": z_down if way == 0 else z_up},
        )
        return zin[way, s, i].astype(F32)

    def z_step(s, first):
        targets = (pair_at(half_z - s), pair_at(s - half_z))
        for j in range(SUB):
            for way in range(2):
                i = j if way == 0 else SUB - 1 - j
                early = j < (UP_SUB if way == 0 else SUB - UP_SUB)
                if early != first:
                    continue
                value = term[targets[way], i]
                if s > 1 or (s == 1 and early):
                    value = value + z_arrive(way, s - 1, i)
                zout[way, s, i] = value.astype(BF16)
                z_send(way, s, i)

    def z_finish():
        for i in range(SUB):
            total = term[place_z, i] + z_arrive(0, half_z - 1, i) + z_arrive(1, half_z - 1, i)
            rows_here = hidden // SUB
            here = pl.ds(i * rows_here, rows_here)
            gd_out[here, :] = (total * (1.0 / n_z)).astype(BF16)
            store = pltpu.make_async_copy(gd_out.at[here, :], gd_hbm.at[here, :], out_sem.at[2 + i])
            store.start()
            stores.append(store)

    def gate_up(q):
        block = row_block(0, q)
        return dot_t(block, weight(gw, q)), dot_t(block, weight(uw, q))

    def act_grad(q):
        return dot_t(row_block(1, q), weight(dw, q))

    def down_part(q):
        put_part(0, q, dot(act_b, weight(dw, q)))

    def input_part(q):
        put_part(1, q, dot(gate_back, weight(gw, q)) + dot(up_back, weight(uw, q)))

    dispatch(0)
    dispatch(1)
    for k in range(2):
        dispatch_wait(0, relay_right[k])
        dispatch_wait(0, relay_left[k])
        gather_start(0, k)
    gather_rest(0, 0)
    gather_rest(0, 1)
    loads[0].wait()
    loads[1].wait()
    gate_s[...], up_s[...] = gate_up(x)
    for k in range(2):
        dispatch_wait(1, relay_right[k])
        dispatch_wait(1, relay_left[k])
        gather_start(1, k)
    pair_send()
    gather_relay(0, 0)
    gather_relay(0, 1)
    gather_rest(1, 0)
    gather_rest(1, 1)
    gather_near(0)
    for q in (left, right):
        gate, up = gate_up(q)
        gate_s[...] += gate
        up_s[...] += up
    gather_relay(1, 0)
    gather_relay(1, 1)
    pair_arrive()
    gather_start(2, 0)
    gather_start(2, 1)
    gather_rest(2, 0)
    gather_rest(2, 1)
    gather_far(0)
    gate, up = gate_up(far)
    gate = gate_s[...] + gate
    up = up_s[...] + up
    squash = 1.0 / (1.0 + jnp.exp(-gate))
    swish = gate * squash
    act = swish * up
    gate_s[...] = up * squash * (1.0 + gate * (1.0 - squash))
    up_s[...] = swish
    act_b = act.astype(BF16)
    acts[0] = act.T.astype(BF16)
    act_send()
    loads[2].wait()
    gather_near(1)
    down_part(far)
    reduce_far(0)
    down_part(right)
    down_part(left)
    gather_relay(2, 0)
    gather_relay(2, 1)
    reduce_near(0)
    grad = act_grad(x) + act_grad(left) + act_grad(right)
    gather_far(1)
    grad = grad + act_grad(far)
    gate_back = (grad * gate_s[...]).astype(BF16)
    up_back = (grad * up_s[...]).astype(BF16)
    input_part(far)
    reduce_far(1)
    act_arrive()
    gather_near(2)
    gather_far(2)
    make_term(pair_at(half_z))
    z_step(0, True)
    make_term(pair_at(half_z - 1))
    make_term(pair_at(1 - half_z))
    z_step(1, False)
    reduce_relay(0)
    input_part(right)
    input_part(left)
    reduce_near(1)
    for s in range(2, half_z):
        make_term(pair_at(half_z - s))
        make_term(pair_at(s - half_z))
    make_term(place_z)
    down_part(x)
    input_part(x)
    reduce_relay(1)
    reduce_end(0)
    z_step(1, True)
    z_step(2, False)
    reduce_end(1)
    z_step(2, True)
    combine(0)
    z_step(3, False)
    combine(1)
    z_step(3, True)
    finish(0)
    finish(1)
    z_finish()
    for store in stores:
        store.wait()
    for copy in started:
        copy.wait_send()


def shards(
    tokens, routes, positions, combine_weights, cotangent, gate_weight, up_weight, down_weight
):
    n_z, n_e, n_x = lax.axis_size("dp"), lax.axis_size("expert"), lax.axis_size("tensor")
    tokens_here, width = tokens.shape
    group_size = routes.shape[0]
    cap = group_size // 2
    hidden = gate_weight.shape[2]
    q_cols = width // n_x
    n_slots = n_e * cap
    per_piece, n_pairs = n_e // PIECES, n_z // 2
    half_z = n_pairs // 2
    pair_chunks = n_pairs // n_x
    z_rows = width // n_z
    hbm = pl.BlockSpec(memory_space=pl.ANY)
    dma = pltpu.SemaphoreType.DMA
    weights = [jnp.swapaxes(w[0], 0, 1) for w in (gate_weight, up_weight, down_weight)]
    plans = [v.T for v in (routes, positions, combine_weights)]
    quarter = (PIECES, per_piece, cap, q_cols)
    slots = (n_e, cap, q_cols)
    return pl.pallas_call(
        functools.partial(kernel, n_z, n_e),
        out_shape=(
            jax.ShapeDtypeStruct((tokens_here, width), BF16),
            jax.ShapeDtypeStruct((tokens_here, width), BF16),
            jax.ShapeDtypeStruct((hidden, z_rows), BF16),
        ),
        in_specs=[hbm] * 8,
        out_specs=(hbm, hbm, hbm),
        scratch_shapes=[pltpu.VMEM(v.shape, v.dtype) for v in (tokens, cotangent, *plans)]
        + [pltpu.VMEM((hidden, width), BF16)] * 3
        + [
            pltpu.VMEM((2, n_x, tokens_here, q_cols), BF16),
            pltpu.VMEM((group_size, q_cols), F32),
            pltpu.VMEM((2,) + slots, BF16),
            pltpu.VMEM((2, n_x) + quarter, BF16),
            pltpu.VMEM((n_slots, hidden), F32),
            pltpu.VMEM((n_slots, hidden), F32),
            pltpu.VMEM((2, n_x) + quarter, BF16),
            pltpu.VMEM((2,) + quarter, BF16),
            pltpu.VMEM((2,) + quarter, BF16),
            pltpu.VMEM((2, 2) + quarter, BF16),
            pltpu.VMEM((2,) + quarter, BF16),
            pltpu.VMEM((2,) + slots, BF16),
            pltpu.VMEM((2, n_x, tokens_here, q_cols), BF16),
            pltpu.VMEM((2, hidden, n_slots), BF16),
            pltpu.VMEM((n_x, pair_chunks, PIECES, per_piece, cap, z_rows), BF16),
            pltpu.VMEM((n_pairs, SUB, hidden // SUB, z_rows), F32),
            pltpu.VMEM((2, half_z, SUB, hidden // SUB, z_rows), BF16),
            pltpu.VMEM((2, half_z, SUB, hidden // SUB, z_rows), BF16),
            pltpu.VMEM((hidden, z_rows), BF16),
            dma((5,)),
            dma((2 + SUB,)),
            dma((3,)),
            dma((2, n_x)),
            dma((2, n_x)),
            dma((2, n_e)),
            dma((2, n_e)),
            dma((3, 2, 2, PIECES)),
            dma((3, 2, 2, PIECES)),
            dma((2, 2, 2, PIECES)),
            dma((2, 2, 2, PIECES)),
            dma((2, n_e)),
            dma((2, n_e)),
            dma((2, n_x)),
            dma((2, n_x)),
            dma((1,)),
            dma((1,)),
            dma((pair_chunks,)),
            dma((pair_chunks,)),
            dma((2, half_z, SUB)),
            dma((2, half_z, SUB)),
        ],
        compiler_params=pltpu.CompilerParams(
            collective_id=0, has_side_effects=True, vmem_limit_bytes=56 * 1024 * 1024
        ),
    )(tokens, cotangent, *plans, *weights)


def place(*refs):
    half = len(refs) // 2
    for source, target in zip(refs[:half], refs[half:]):
        target[...] = source[...]


def body(*arrays):
    results = shards(*arrays)
    layer_out, grad_tokens, grad_down = pl.pallas_call(
        place,
        out_shape=tuple(jax.ShapeDtypeStruct(r.shape, r.dtype) for r in results),
        in_specs=[pl.BlockSpec(memory_space=pltpu.VMEM)] * 3,
        out_specs=(pl.BlockSpec(memory_space=pltpu.VMEM),) * 3,
    )(*results)
    return layer_out, grad_tokens, jnp.swapaxes(grad_down, 0, 1)[None]


def solution(mesh):
    return jax.shard_map(
        body,
        mesh=mesh,
        in_specs=(
            P(("dp", "expert", "tensor"), None),
            P(("dp", "expert"), None),
            P(("dp", "expert"), None),
            P(("dp", "expert"), None),
            P(("dp", "expert", "tensor"), None),
            P("expert", None, "tensor"),
            P("expert", None, "tensor"),
            P("expert", None, "tensor"),
        ),
        out_specs=(
            P(("dp", "expert", "tensor"), None),
            P(("dp", "expert", "tensor"), None),
            P("expert", "dp", "tensor"),
        ),
        check_vma=False,
    )
```
